32 devices in a mesh: clip: 2 (over y), frame: 4 (over z), track: 4 (over x, core).
Axes of the slice: x: 2, y: 2, z: 4, core: 2. Of those that a mesh axis runs over, the one named last changes fastest.
Arguments:
- feature_maps: bfloat16 [8, 4096, 256], P(('clip', 'frame')), parts along dimension 0, may hold values from -6 to 6
- query_frame: int32 [1024], P('clip'), parts along dimension 0, may hold values from 0 to 3
- query_row: int32 [1024], P('clip'), parts along dimension 0, may hold values from 0 to 63
- query_col: int32 [1024], P('clip'), parts along dimension 0, may hold values from 0 to 63
- track_order: int32 [1024], P('clip'), parts along dimension 0, may hold values from 0 to 511, each once
- conv_weight: float32 [16, 9], replicated, may hold values from -2 to 2
- conv_bias: float32 [16], replicated, may hold values from -2 to 2
- head_weight: float32 [16], replicated, may hold values from -2 to 2
- mix_in: bfloat16 [256, 1024], replicated, may hold values from -0.375 to 0.375
- temporal_taps: float32 [3, 1024], replicated, may hold values from -2.5 to 2.5
- mix_gain: float32 [1024], replicated, may hold values from 0.25 to 1.75
- mix_out: bfloat16 [1024, 3], replicated, may hold values from -0.1875 to 0.1875
Outputs:
- estimates: float32 [1024, 3, 4], P(('clip', 'frame', 'track')), parts along dimension 0
The draws below stay inside these ranges and needn't reach their ends.
There are 2 independent parts, one for each index of `clip`. The reference program is written for one: setup_inputs(seed, part) draws one part's arguments, and reference() takes and returns one part's arrays. A program takes and returns all parts, laid end to end along the dimension named above; an argument that names none is the same for every part. Nothing has to cross between parts.
Inputs may be any that keep to these rules, and one draw needn't show every extreme that they name: `track_order`: each track appears in exactly one slot.
All inputs are finite; a program needn't handle non-finite values.
Results may differ from the reference program's by a relative error of at most 0.0053.
Values may be sent and summed in bfloat16 or wider, within the bound.
No kernel may reach another device: no remote copies, remote signals or barrier semaphores. Data moves between devices by JAX's collectives and lax.ppermute only.
A program may use at most 64 MiB of HBM per device.

```python
import math
import jax
import jax.numpy as jnp
import numpy as np
from jax import lax

CHAN = 256
GRID_H = 64
GRID_W = 64
MIXW = 1024
HID = 16
FRAMES = 4
NTRACK = 512


def place_ends(values, rng, low, high):
    index_at = [jax.random.randint(jax.random.fold_in(rng, axis), (), 0, length) for axis, length in enumerate(values.shape)]
    main_axis = values.shape.index(max(values.shape))
    neighbour = index_at[:main_axis] + [(index_at[main_axis] + 1) % values.shape[main_axis]] + index_at[main_axis + 1:]
    return values.at[tuple(index_at)].set(low).at[tuple(neighbour)].set(high)


def shard_levels(key, dims, pieces, low, top_value):
    def one(axis_at, blocks):
        steps = jax.random.uniform(jax.random.fold_in(jax.random.fold_in(key, 6), axis_at), (blocks,), jnp.float32, low / len(pieces), top_value / len(pieces))
        return jnp.repeat(jnp.exp(steps), dims[axis_at] // blocks).reshape((-1,) + (1,) * (len(dims) - axis_at - 1))

    factor_of = one(*pieces[0])
    for cut in pieces[1:]:
        factor_of = factor_of * one(*cut)
    return factor_of


def cumulative_ranks(number_of, slope):
    loads = [(1 << 20) // math.isqrt(grade ** slope) + 1 for grade in range(1, number_of + 1)]
    scale = 1 + sum(loads) // (1 << 30)
    return np.cumsum(np.array([max(1, weight // scale) for weight in loads]))


def ranked(own_key, extent, amount, slope):
    listing = cumulative_ranks(amount, slope)
    ticket = jax.random.randint(jax.random.fold_in(own_key, 1), extent, 0, int(listing[amount - 1]))
    standing = jnp.searchsorted(jnp.asarray(listing, jnp.int32), ticket, side="right")
    return jax.random.permutation(jax.random.fold_in(own_key, 2), amount)[standing].astype(jnp.int32)


def centred(stream_key, dims, scale, reach, cuts=(), kind=jnp.bfloat16):
    result = jax.random.normal(stream_key, dims, jnp.float32) * scale
    if len(cuts) > 0:
        result = shard_levels(stream_key, dims, cuts, -0.22, 0.18) * result
    return jnp.clip(result, min=-reach, max=reach).astype(kind)


def setup_inputs(seed: int = 0, part: int = 0) -> dict:
    seeds = jax.random.split(jax.random.key(seed), 13)
    part_splits = jax.random.split(jax.random.fold_in(seeds[12], part), 13)
    return {
        "feature_maps": centred(part_splits[0], (FRAMES, GRID_H * GRID_W, CHAN), 1.0, 6.0, ((0, 4),)),
        "query_frame": place_ends(ranked(part_splits[1], (NTRACK,), FRAMES, 2), jax.random.fold_in(part_splits[1], 3), 0, FRAMES - 1).astype(jnp.int32),
        "query_row": place_ends(jax.random.randint(part_splits[2], (NTRACK,), 0, GRID_H), jax.random.fold_in(part_splits[2], 1), 0, GRID_H - 1).astype(jnp.int32),
        "query_col": place_ends(jax.random.randint(part_splits[3], (NTRACK,), 0, GRID_W), jax.random.fold_in(part_splits[3], 1), 0, GRID_W - 1).astype(jnp.int32),
        "track_order": jax.random.permutation(part_splits[4], NTRACK).astype(jnp.int32),
        "conv_weight": centred(seeds[5], (HID, 9), 0.4, 2.0, (), jnp.float32),
        "conv_bias": centred(seeds[6], (HID,), 0.5, 2.0, (), jnp.float32),
        "head_weight": centred(seeds[7], (HID,), 0.5, 2.0, (), jnp.float32),
        "mix_in": centred(seeds[8], (CHAN, MIXW), CHAN ** -0.5, 0.375),
        "temporal_taps": centred(seeds[9], (3, MIXW), 0.6, 2.5, (), jnp.float32),
        "mix_gain": jnp.clip(1.0 + 0.15 * jax.random.normal(seeds[10], (MIXW,), jnp.float32), 0.25, 1.75),
        "mix_out": centred(seeds[11], (MIXW, 3), MIXW ** -0.5, 0.1875),
    }


def conv_logits(cost, conv_weight, conv_bias, head_weight):
    height, width = (cost.shape[1], cost.shape[2])
    padded = jnp.pad(cost, ((0, 0), (1, 1), (1, 1)))
    logit = jnp.zeros(cost.shape, jnp.float32)
    for channel in range(conv_weight.shape[0]):
        acc = jnp.zeros(cost.shape, jnp.float32) + conv_bias[channel]
        for tap in range(9):
            acc = acc + conv_weight[channel, tap] * padded[:, tap // 3:tap // 3 + height, tap % 3:tap % 3 + width]
        logit = logit + head_weight[channel] * jax.nn.relu(acc)
    return logit

def block_terms(qblock, maps, conv_weight, conv_bias, head_weight, row_pos, col_pos):
    cost = lax.dot_general(qblock, maps, (((1,), (1,)), ((), ())), preferred_element_type=jnp.float32)
    cost = cost * (1.0 / math.sqrt(maps.shape[1]))
    logit = conv_logits(cost.reshape(cost.shape[0], GRID_H, GRID_W), conv_weight, conv_bias, head_weight)
    heat = jax.nn.softmax(logit.reshape(cost.shape), axis=-1)
    row_est = lax.optimization_barrier(jnp.sum(heat * row_pos, axis=-1)).astype(jnp.bfloat16)
    col_est = lax.optimization_barrier(jnp.sum(heat * col_pos, axis=-1)).astype(jnp.bfloat16)
    sampled = jnp.dot(heat.astype(jnp.bfloat16), maps, preferred_element_type=jnp.float32).astype(jnp.bfloat16)
    return (sampled, row_est, col_est)

def temporal_mix(extended, temporal_taps, mix_gain, mix_out):
    mixed = temporal_taps[0] * extended[:, :-2] + temporal_taps[1] * extended[:, 1:-1] + temporal_taps[2] * extended[:, 2:]
    normed = mixed * lax.rsqrt(lax.optimization_barrier(jnp.mean(mixed * mixed, axis=-1, keepdims=True)) + 1e-06) * mix_gain
    hidden = jax.nn.gelu(normed).astype(jnp.bfloat16)
    rows, frames_here = (hidden.shape[0], hidden.shape[1])
    delta = jnp.dot(hidden.reshape(rows * frames_here, hidden.shape[2]), mix_out, preferred_element_type=jnp.float32)
    return delta.reshape(rows, frames_here, 3)

def assemble(row_est, col_est, delta):
    return jnp.stack([row_est.astype(jnp.float32) + delta[:, :, 0], col_est.astype(jnp.float32) + delta[:, :, 1], delta[:, :, 2]], axis=1)

def reference(feature_maps, query_frame, query_row, query_col, track_order, conv_weight, conv_bias, head_weight, mix_in, temporal_taps, mix_gain, mix_out):
    pixels = GRID_H * GRID_W
    frame_ids = query_frame[track_order]
    pixel_ids = query_row[track_order] * GRID_W + query_col[track_order]
    flat = (frame_ids * pixels + pixel_ids).astype(jnp.int32)
    queries = feature_maps.reshape(FRAMES * pixels, CHAN)[flat]
    positions = jnp.arange(pixels, dtype=jnp.int32)
    row_pos = (positions // GRID_W).astype(jnp.float32) / (GRID_H - 1)
    col_pos = (positions % GRID_W).astype(jnp.float32) / (GRID_W - 1)
    blk = min(NTRACK, 64)
    blocks = NTRACK // blk

    def per_block(qblock):

        def per_frame(maps):
            return block_terms(qblock, maps, conv_weight, conv_bias, head_weight, row_pos, col_pos)
        return lax.map(per_frame, feature_maps)
    sampled, row_est, col_est = lax.map(per_block, queries.reshape(blocks, blk, CHAN))
    sampled = jnp.transpose(sampled, (0, 2, 1, 3)).reshape(NTRACK, FRAMES, CHAN)
    row_est = jnp.transpose(row_est, (0, 2, 1)).reshape(NTRACK, FRAMES)
    col_est = jnp.transpose(col_est, (0, 2, 1)).reshape(NTRACK, FRAMES)
    projected = jnp.dot(sampled.reshape(NTRACK * FRAMES, CHAN), mix_in, preferred_element_type=jnp.float32)
    projected = projected.reshape(NTRACK, FRAMES, MIXW)
    extended = jnp.pad(projected, ((0, 0), (1, 1), (0, 0)))
    delta = temporal_mix(extended, temporal_taps, mix_gain, mix_out)
    return assemble(row_est, col_est, delta)
```

```python
import functools
import math

import jax
import jax.numpy as jnp
from jax import lax
from jax.experimental import pallas as pl
from jax.experimental.pallas import tpu as pltpu
from jax.sharding import PartitionSpec as P

GRID_H = 64
GRID_W = 64
TILE = 16
KDIM = 256
ROWS_PAD = GRID_H + 4
LANES = 128

VMEM_SPEC = pl.BlockSpec(memory_space=pltpu.VMEM)
SMEM_SPEC = pl.BlockSpec(memory_space=pltpu.SMEM)
F32 = jnp.float32
BF16 = jnp.bfloat16


def iota(shape, dim):
    return lax.broadcasted_iota(jnp.int32, shape, dim)


def pick_kernel(frame_ref, tracks_ref, qf_ref, qr_ref, qc_ref, maps_ref, out_ref):
    total = qf_ref.shape[1]
    slots = tracks_ref.shape[1]
    pixels = maps_ref.shape[0]
    hot = jnp.where(iota((total, slots), 0) == tracks_ref[...], 1.0, 0.0).astype(BF16)
    table = jnp.concatenate(
        [qf_ref[...], qr_ref[...], qc_ref[...], jnp.zeros((5, total), jnp.int32)], axis=0
    ).astype(F32).astype(BF16)
    found = jnp.dot(table, hot, preferred_element_type=F32)
    local = found[0:1] - frame_ref[0].astype(F32)
    flat = jnp.where(local == 0.0, found[1:2] * GRID_W + found[2:3], -1.0)
    column = jnp.broadcast_to(flat, (slots, slots)).T[:, 0:1].astype(jnp.int32)
    step = 512
    acc = jnp.zeros((slots, maps_ref.shape[1]), F32)
    for base in range(0, pixels, step):
        sel = jnp.where(iota((slots, step), 1) + base == column, 1.0, 0.0).astype(BF16)
        acc = acc + jnp.dot(sel, maps_ref[base : base + step, :], preferred_element_type=F32)
    out_ref[...] = acc.astype(BF16)


def prep_kernel(weight_ref, maps_ref, out_ref, turned_ref):
    hid = weight_ref.shape[0]
    part = 2 * TILE
    row = iota((part, KDIM), 0)
    kk = iota((part, KDIM), 1)
    row_out, col_out = row // TILE, row % TILE
    mid = kk < 12 * TILE
    within = kk % (4 * TILE)
    seg = kk // (4 * TILE)
    edge = kk - 12 * TILE
    edge_seg = edge // TILE
    edge_at = edge % TILE
    use_low = jnp.where(mid, seg, edge_seg) == 2
    for parity in range(2):
        row_in = jnp.where(mid, within // TILE, edge_at % 8 - 2 * parity)
        col_in = jnp.where(mid, within % TILE, jnp.where(edge_at < 8, -1, TILE))
        down, across = row_in - row_out, col_in - col_out + 1
        good = (row_in >= 0) & (row_in < 4) & (down >= 0) & (down < 3)
        good = good & (across >= 0) & (across < 3) & (mid | (edge_seg < 3))
        tap = jnp.where(good, down * 3 + across, -1)
        masks = [tap == t for t in range(9)]
        for h in range(hid):
            full = jnp.zeros((part, KDIM), F32)
            for t in range(9):
                full = jnp.where(masks[t], weight_ref[h, t], full)
            high = full.astype(BF16).astype(F32)
            value = jnp.where(use_low, full - high, high)
            out_ref[parity, h * part : (h + 1) * part, :] = value.astype(BF16)
    step = 512
    for base in range(0, maps_ref.shape[0], step):
        turned_ref[:, base : base + step] = maps_ref[base : base + step, :].T


def heat_kernel(
    pieces,
    bias_ref,
    head_ref,
    *refs,
):
    q_refs = refs[:pieces]
    maps_ref, turned_ref, weight_ref, out_ref = refs[pieces : pieces + 4]
    cost_ref, high_ref, low_ref, edge_high, edge_low, logit_ref, heat_ref = refs[pieces + 4 :]
    pixels, chan = maps_ref.shape
    slots = q_refs[0].shape[0]
    hid = bias_ref.shape[0]
    part = 2 * TILE
    query = q_refs[0][...].astype(F32)
    for ref in q_refs[1:]:
        query = query + ref[...].astype(F32)
    turned_q = query.T.astype(BF16)
    scale = 1.0 / math.sqrt(chan)

    for lo, hi in ((0, GRID_W), (GRID_W + pixels, ROWS_PAD * GRID_W)):
        cost_ref[lo:hi, :] = jnp.zeros((hi - lo, slots), F32)
        high_ref[lo:hi, :] = jnp.zeros((hi - lo, slots), BF16)
        low_ref[lo:hi, :] = jnp.zeros((hi - lo, slots), BF16)

    step = 256

    def cost_step(n, carry):
        at = pl.multiple_of(n * step, step)
        cost = jnp.dot(maps_ref[pl.ds(at, step), :], turned_q, preferred_element_type=F32) * scale
        to = pl.multiple_of(at + GRID_W, GRID_W)
        high = cost.astype(BF16)
        cost_ref[pl.ds(to, step), :] = cost
        high_ref[pl.ds(to, step), :] = high
        low_ref[pl.ds(to, step), :] = (cost - high.astype(F32)).astype(BF16)
        return carry

    lax.fori_loop(0, pixels // step, cost_step, 0)

    cols = GRID_W // TILE
    const = 0.0
    for h in range(hid):
        const = const + head_ref[h] * bias_ref[h]

    def window_step(j, best):
        for k in range(cols):
            base = j * 4 * GRID_W + k * TILE
            left = (
                jnp.zeros((8, slots), F32)
                if k == 0
                else cost_ref[pl.ds(base - 1, 8, stride=GRID_W), :]
            )
            right = (
                jnp.zeros((8, slots), F32)
                if k == cols - 1
                else cost_ref[pl.ds(base + TILE, 8, stride=GRID_W), :]
            )
            both = jnp.concatenate([left, right], axis=0)
            high = both.astype(BF16)
            edge_high[k] = high
            edge_low[k] = (both - high.astype(F32)).astype(BF16)
        for parity in range(2):
            top = (4 * j + 2 * parity) * GRID_W
            for pair in range(cols // 2):
                sides = []
                for k in (2 * pair, 2 * pair + 1):
                    at = [pl.multiple_of(top + rr * GRID_W + k * TILE, TILE) for rr in range(4)]
                    mid_high = [high_ref[pl.ds(a, TILE), :] for a in at]
                    mid_low = [low_ref[pl.ds(a, TILE), :] for a in at]
                    eh, el = edge_high[k], edge_low[k]
                    sides.append(
                        jnp.concatenate(mid_high + mid_low + mid_high + [eh, el, eh, eh], axis=0)
                    )
                window = jnp.concatenate(sides, axis=1)
                act = jnp.dot(weight_ref[parity], window, preferred_element_type=F32)
                acc = jnp.full((part, 2 * slots), const, F32)
                for h in range(hid):
                    acc = acc + head_ref[h] * jnp.maximum(
                        act[h * part : (h + 1) * part], -bias_ref[h]
                    )
                for side in range(2):
                    k = 2 * pair + side
                    for rr in range(2):
                        piece = acc[rr * TILE : (rr + 1) * TILE, side * slots : (side + 1) * slots]
                        to = pl.multiple_of(top + rr * GRID_W + k * TILE, TILE)
                        logit_ref[pl.ds(to, TILE), :] = piece
                        best = jnp.maximum(best, jnp.maximum(piece[:8], piece[8:]))
        return best

    best = lax.fori_loop(0, GRID_H // 4, window_step, jnp.full((8, slots), -jnp.inf, F32))
    top_value = jnp.max(best, axis=0, keepdims=True)

    def exp_step(r, carry):
        row_acc, col_acc = carry
        at = pl.multiple_of(r * GRID_W, GRID_W)
        value = jnp.exp(logit_ref[pl.ds(at, GRID_W), :] - top_value)
        logit_ref[pl.ds(at, GRID_W), :] = value
        col_acc = col_acc + value
        folded = value[0:8]
        for n in range(1, GRID_W // 8):
            folded = folded + value[8 * n : 8 * n + 8]
        row_acc = row_acc + folded * (r.astype(F32) * (1.0 / (GRID_H - 1)))
        return row_acc, col_acc

    row_acc, col_acc = lax.fori_loop(
        0, GRID_H, exp_step, (jnp.zeros((8, slots), F32), jnp.zeros((GRID_W, slots), F32))
    )
    total = jnp.sum(col_acc, axis=0, keepdims=True)
    inverse = 1.0 / total
    row_est = jnp.sum(row_acc, axis=0, keepdims=True) * inverse
    col_pos = iota((GRID_W, slots), 0).astype(F32) * (1.0 / (GRID_W - 1))
    col_est = jnp.sum(col_acc * col_pos, axis=0, keepdims=True) * inverse

    def norm_step(n, carry):
        at = pl.multiple_of(n * step, step)
        heat_ref[pl.ds(at, step), :] = (logit_ref[pl.ds(at, step), :] * inverse).astype(BF16)
        return carry

    lax.fori_loop(0, pixels // step, norm_step, 0)
    sampled = jnp.dot(turned_ref[...], heat_ref[...], preferred_element_type=F32)
    rest = jnp.concatenate([row_est, col_est, jnp.zeros((LANES - 2, slots), F32)], axis=0)
    out_ref[:, :chan] = sampled.T.astype(BF16)
    out_ref[:, chan:] = rest.T.astype(BF16)


def mix_kernel(got_ref, mix_in_ref, taps_ref, gain_ref, mix_out_ref, out_ref, z_ref):
    frames, rows, width = got_ref.shape
    chan = mix_in_ref.shape[0]
    for t in range(frames):
        z_ref[t] = jnp.dot(got_ref[t, :, :chan], mix_in_ref[...], preferred_element_type=F32)
    for t in range(frames):
        mixed = taps_ref[1:2, :] * z_ref[t]
        if t > 0:
            mixed = taps_ref[0:1, :] * z_ref[t - 1] + mixed
        if t < frames - 1:
            mixed = mixed + taps_ref[2:3, :] * z_ref[t + 1]
        power = jnp.mean(mixed * mixed, axis=-1, keepdims=True)
        normed = mixed * lax.rsqrt(power + 1e-06) * gain_ref[...]
        hidden = jax.nn.gelu(normed).astype(BF16)
        delta = jnp.dot(hidden, mix_out_ref[...], preferred_element_type=F32)
        place = got_ref[t, :, chan:].astype(F32)
        out_ref[t] = delta + place


def on_device(
    feature_maps,
    query_frame,
    query_row,
    query_col,
    track_order,
    conv_weight,
    conv_bias,
    head_weight,
    mix_in,
    temporal_taps,
    mix_gain,
    mix_out,
):
    frame_count = lax.axis_size("frame")
    track_count = lax.axis_size("track")
    frame_here = lax.axis_index("frame").astype(jnp.int32)
    track_here = lax.axis_index("track")
    f_dev, pixels, chan = feature_maps.shape
    total = track_order.shape[0]
    tr_dev = total // track_count
    sub_rows = tr_dev // frame_count
    hid = conv_weight.shape[0]
    mixw = mix_in.shape[1]
    maps = feature_maps.reshape(f_dev * pixels, chan)

    tracks = lax.dynamic_index_in_dim(
        track_order.reshape(frame_count, track_count, sub_rows), track_here, 1, keepdims=False
    ).reshape(1, tr_dev)

    picks = pl.pallas_call(
        pick_kernel,
        name="pick",
        out_shape=jax.ShapeDtypeStruct((tr_dev, chan), BF16),
        in_specs=[SMEM_SPEC] + [VMEM_SPEC] * 5,
        out_specs=VMEM_SPEC,
    )(
        frame_here.reshape(1),
        tracks,
        query_frame.reshape(1, total),
        query_row.reshape(1, total),
        query_col.reshape(1, total),
        maps,
    )
    pieces = [picks]
    for shift in range(1, frame_count):
        pieces.append(
            lax.ppermute(picks, "frame", [(i, (i + shift) % frame_count) for i in range(frame_count)])
        )

    part = 2 * TILE
    weight, turned = pl.pallas_call(
        prep_kernel,
        name="prep",
        out_shape=(
            jax.ShapeDtypeStruct((2, hid * part, KDIM), BF16),
            jax.ShapeDtypeStruct((chan, pixels), BF16),
        ),
        in_specs=[SMEM_SPEC, VMEM_SPEC],
        out_specs=(VMEM_SPEC, VMEM_SPEC),
    )(conv_weight, maps)

    padded = ROWS_PAD * GRID_W
    packed = pl.pallas_call(
        functools.partial(heat_kernel, frame_count),
        name="heat",
        out_shape=jax.ShapeDtypeStruct((tr_dev, chan + LANES), BF16),
        in_specs=[SMEM_SPEC] * 2 + [VMEM_SPEC] * (frame_count + 3),
        out_specs=VMEM_SPEC,
        scratch_shapes=[
            pltpu.VMEM((padded, tr_dev), F32),
            pltpu.VMEM((padded, tr_dev), BF16),
            pltpu.VMEM((padded, tr_dev), BF16),
            pltpu.VMEM((GRID_W // TILE, TILE, tr_dev), BF16),
            pltpu.VMEM((GRID_W // TILE, TILE, tr_dev), BF16),
            pltpu.VMEM((pixels, tr_dev), F32),
            pltpu.VMEM((pixels, tr_dev), BF16),
        ],
    )(conv_bias, head_weight, *pieces, maps, turned, weight)

    got = lax.all_to_all(
        packed.reshape(frame_count, sub_rows, chan + LANES),
        "frame",
        split_axis=0,
        concat_axis=0,
        tiled=True,
    )
    wide_out = jnp.pad(mix_out, ((0, 0), (0, LANES - mix_out.shape[1])))
    mixed = pl.pallas_call(
        mix_kernel,
        name="mix",
        out_shape=jax.ShapeDtypeStruct((frame_count, sub_rows, LANES), F32),
        in_specs=[VMEM_SPEC] * 5,
        out_specs=VMEM_SPEC,
        scratch_shapes=[pltpu.VMEM((frame_count, sub_rows, mixw), F32)],
    )(got, mix_in, temporal_taps, mix_gain.reshape(1, mixw), wide_out)
    return jnp.transpose(mixed[:, :, :3], (1, 2, 0))


def solution(mesh):
    placed = (
        P(("clip", "frame"), None, None),
        P("clip"),
        P("clip"),
        P("clip"),
        P("clip"),
        P(),
        P(),
        P(),
        P(),
        P(),
        P(),
        P(),
    )
    return jax.shard_map(
        on_device,
        mesh=mesh,
        in_specs=placed,
        out_specs=P(("clip", "frame", "track"), None, None),
        check_vma=False,
    )
```

```python
import functools
import math

import jax
import jax.numpy as jnp
from jax import lax
from jax.experimental import pallas as pl
from jax.experimental.pallas import tpu as pltpu
from jax.sharding import PartitionSpec as P

GRID_H = 64
GRID_W = 64
TILE = 16
KDIM = 256
ROWS_PAD = GRID_H + 4
LANES = 128

VMEM_SPEC = pl.BlockSpec(memory_space=pltpu.VMEM)
SMEM_SPEC = pl.BlockSpec(memory_space=pltpu.SMEM)
F32 = jnp.float32
BF16 = jnp.bfloat16


def iota(shape, dim):
    return lax.broadcasted_iota(jnp.int32, shape, dim)


def pick_kernel(
    frame_count,
    track_count,
    place_ref,
    order_ref,
    qf_ref,
    qr_ref,
    qc_ref,
    maps_ref,
    out_ref,
    held_ref,
    sem,
):
    total = order_ref.shape[1]
    slots = out_ref.shape[0]
    pixels, chan = held_ref.shape
    chunks = sem.shape[0]
    step = pixels // chunks
    copies = [
        pltpu.make_async_copy(
            maps_ref.at[pl.ds(n * step, step)], held_ref.at[pl.ds(n * step, step)], sem.at[n]
        )
        for n in range(chunks)
    ]
    for copy in copies:
        copy.start()
    frame_here, track_here = place_ref[0], place_ref[1]
    sub = slots // frame_count
    at = iota((1, slots), 1)
    slot = (at // sub * track_count + track_here) * sub + at % sub
    row = iota((total, slots), 0)
    hot = jnp.where(row == slot, 1.0, 0.0).astype(BF16)
    order = order_ref[...]
    blank = jnp.zeros((5, total), jnp.int32)
    table = jnp.concatenate([order // 256, order % 256, blank, blank[:1]], axis=0)
    found = jnp.dot(table.astype(F32).astype(BF16), hot, preferred_element_type=F32)
    track = (found[0:1] * 256.0 + found[1:2]).astype(jnp.int32)
    hot = jnp.where(row == track, 1.0, 0.0).astype(BF16)
    table = jnp.concatenate([qf_ref[...], qr_ref[...], qc_ref[...], blank], axis=0)
    found = jnp.dot(table.astype(F32).astype(BF16), hot, preferred_element_type=F32)
    flat = found[1:2] * GRID_W + found[2:3]
    flat = jnp.where(found[0:1] == frame_here.astype(F32), flat, -1.0)
    column = jnp.broadcast_to(flat, (slots, slots)).T[:, 0:1].astype(jnp.int32)
    acc = jnp.zeros((slots, chan), F32)
    for n in range(chunks):
        sel = jnp.where(iota((slots, step), 1) + n * step == column, 1.0, 0.0).astype(BF16)
        copies[n].wait()
        acc = acc + jnp.dot(
            sel, held_ref[n * step : (n + 1) * step, :], preferred_element_type=F32
        )
    out_ref[...] = acc.astype(BF16)


def prep_kernel(weight_ref, out_ref):
    hid = weight_ref.shape[0]
    part = 2 * TILE
    row = iota((part, KDIM), 0)
    kk = iota((part, KDIM), 1)
    row_out, col_out = row // TILE, row % TILE
    mid = kk < 12 * TILE
    within = kk % (4 * TILE)
    seg = kk // (4 * TILE)
    edge = kk - 12 * TILE
    edge_seg = edge // TILE
    edge_at = edge % TILE
    use_low = jnp.where(mid, seg, edge_seg) == 2
    for parity in range(2):
        row_in = jnp.where(mid, within // TILE, edge_at % 8 - 2 * parity)
        col_in = jnp.where(mid, within % TILE, jnp.where(edge_at < 8, -1, TILE))
        down, across = row_in - row_out, col_in - col_out + 1
        good = (row_in >= 0) & (row_in < 4) & (down >= 0) & (down < 3)
        good = good & (across >= 0) & (across < 3) & (mid | (edge_seg < 3))
        tap = jnp.where(good, down * 3 + across, -1)
        masks = [tap == t for t in range(9)]
        for h in range(hid):
            full = jnp.zeros((part, KDIM), F32)
            for t in range(9):
                full = jnp.where(masks[t], weight_ref[h, t], full)
            high = full.astype(BF16).astype(F32)
            value = jnp.where(use_low, full - high, high)
            out_ref[parity, h * part : (h + 1) * part, :] = value.astype(BF16)


def heat_kernel(
    pieces,
    order,
    frame_ref,
    bias_ref,
    head_ref,
    *refs,
):
    q_refs = refs[:pieces]
    maps_ref, weight_ref = refs[pieces : pieces + 2]
    out_refs = refs[pieces + 2 : 2 * pieces + 2]
    cost_ref, high_ref, low_ref, edge_high, edge_low, logit_ref, full_ref = refs[2 * pieces + 2 :]
    pixels, chan = maps_ref.shape
    slots = q_refs[0].shape[0]
    hid = bias_ref.shape[0]
    part = 2 * TILE
    query = q_refs[0][...].astype(F32)
    for ref in q_refs[1:]:
        query = query + ref[...].astype(F32)
    turned_q = query.T.astype(BF16)
    scale = 1.0 / math.sqrt(chan)

    for lo, hi in ((0, GRID_W), (GRID_W + pixels, ROWS_PAD * GRID_W)):
        cost_ref[lo:hi, :] = jnp.zeros((hi - lo, slots), F32)
        high_ref[lo:hi, :] = jnp.zeros((hi - lo, slots), BF16)
        low_ref[lo:hi, :] = jnp.zeros((hi - lo, slots), BF16)

    step = 512

    def cost_step(n, carry):
        at = pl.multiple_of(n * step, step)
        cost = jnp.dot(maps_ref[pl.ds(at, step), :], turned_q, preferred_element_type=F32) * scale
        to = pl.multiple_of(at + GRID_W, GRID_W)
        high = cost.astype(BF16)
        cost_ref[pl.ds(to, step), :] = cost
        high_ref[pl.ds(to, step), :] = high
        low_ref[pl.ds(to, step), :] = (cost - high.astype(F32)).astype(BF16)
        return carry

    lax.fori_loop(0, pixels // step, cost_step, 0)

    cols = GRID_W // TILE
    const = 0.0
    for h in range(hid):
        const = const + head_ref[h] * bias_ref[h]

    def window_step(j, best):
        for k in range(cols):
            base = j * 4 * GRID_W + k * TILE
            left = (
                jnp.zeros((8, slots), F32)
                if k == 0
                else cost_ref[pl.ds(base - 1, 8, stride=GRID_W), :]
            )
            right = (
                jnp.zeros((8, slots), F32)
                if k == cols - 1
                else cost_ref[pl.ds(base + TILE, 8, stride=GRID_W), :]
            )
            both = jnp.concatenate([left, right], axis=0)
            high = both.astype(BF16)
            edge_high[k] = high
            edge_low[k] = (both - high.astype(F32)).astype(BF16)
        for parity in range(2):
            top = (4 * j + 2 * parity) * GRID_W
            for pair in range(cols // 2):
                sides = []
                for k in (2 * pair, 2 * pair + 1):
                    at = [pl.multiple_of(top + rr * GRID_W + k * TILE, TILE) for rr in range(4)]
                    mid_high = [high_ref[pl.ds(a, TILE), :] for a in at]
                    mid_low = [low_ref[pl.ds(a, TILE), :] for a in at]
                    eh, el = edge_high[k], edge_low[k]
                    sides.append(
                        jnp.concatenate(mid_high + mid_low + mid_high + [eh, el, eh, eh], axis=0)
                    )
                window = jnp.concatenate(sides, axis=1)
                act = jnp.dot(weight_ref[parity], window, preferred_element_type=F32)
                acc = jnp.full((part, 2 * slots), const, F32)
                for h in range(hid):
                    acc = acc + head_ref[h] * jnp.maximum(
                        act[h * part : (h + 1) * part], -bias_ref[h]
                    )
                for side in range(2):
                    k = 2 * pair + side
                    for rr in range(2):
                        piece = acc[rr * TILE : (rr + 1) * TILE, side * slots : (side + 1) * slots]
                        to = pl.multiple_of(top + rr * GRID_W + k * TILE, TILE)
                        logit_ref[pl.ds(to, TILE), :] = piece
                        best = jnp.maximum(best, jnp.maximum(piece[:8], piece[8:]))
        return best

    best = lax.fori_loop(0, GRID_H // 4, window_step, jnp.full((8, slots), -jnp.inf, F32))
    top_value = jnp.max(best, axis=0, keepdims=True)

    def exp_step(n, carry):
        row_acc, col_acc = carry
        for m in range(4):
            r = n * 4 + m
            at = pl.multiple_of(r * GRID_W, GRID_W)
            value = jnp.exp(logit_ref[pl.ds(at, GRID_W), :] - top_value)
            logit_ref[pl.ds(at, GRID_W), :] = value
            col_acc = col_acc + value
            parts = [value[8 * n : 8 * n + 8] for n in range(GRID_W // 8)]
            while len(parts) > 1:
                parts = [a + b for a, b in zip(parts[::2], parts[1::2])]
            row_acc = row_acc + parts[0] * (r.astype(F32) * (1.0 / (GRID_H - 1)))
        return row_acc, col_acc

    row_acc, col_acc = lax.fori_loop(
        0, GRID_H // 4, exp_step, (jnp.zeros((8, slots), F32), jnp.zeros((GRID_W, slots), F32))
    )
    total = jnp.sum(col_acc, axis=0, keepdims=True)
    inverse = 1.0 / total
    row_est = jnp.sum(row_acc, axis=0, keepdims=True) * inverse
    col_pos = iota((GRID_W, slots), 0).astype(F32) * (1.0 / (GRID_W - 1))
    col_est = jnp.sum(col_acc * col_pos, axis=0, keepdims=True) * inverse

    def sample_step(n, acc):
        at = pl.multiple_of(n * step, step)
        heat = (logit_ref[pl.ds(at, step), :] * inverse).astype(BF16)
        return acc + jnp.dot(heat.T, maps_ref[pl.ds(at, step), :], preferred_element_type=F32)

    sampled = lax.fori_loop(0, pixels // step, sample_step, jnp.zeros((slots, chan), F32))
    rest = jnp.concatenate([row_est, col_est, jnp.zeros((LANES - 2, slots), F32)], axis=0)
    sub = slots // pieces
    full_ref[:, :, :chan] = sampled.astype(BF16).reshape(pieces, sub, chan)
    full_ref[:, :, chan:] = rest.T.astype(BF16).reshape(pieces, sub, LANES)
    for m in range(pieces):
        out_refs[m][...] = full_ref[peer(order, frame_ref[0], m, pieces)]


def mix_kernel(order, frames, frame_ref, *refs):
    got_refs = refs[:frames]
    mix_in_ref, taps_ref, gain_ref, mix_out_ref, out_ref, z_ref, place_ref = refs[frames:]
    chan = mix_in_ref.shape[0]
    rows = got_refs[0].shape[0]
    joined = jnp.concatenate([ref[...] for ref in got_refs], axis=0)
    z = jnp.dot(joined[:, :chan], mix_in_ref[...], preferred_element_type=F32)
    for m in range(frames):
        source = peer(order, frame_ref[0], -m, frames)
        z_ref[source] = z[m * rows : (m + 1) * rows]
        place_ref[source] = got_refs[m][:, chan:]
    place = place_ref[...].astype(F32).reshape(frames * rows, LANES).T[:8]
    hidden = []
    for t in range(frames):
        mixed = taps_ref[1:2, :] * z_ref[t]
        if t > 0:
            mixed = taps_ref[0:1, :] * z_ref[t - 1] + mixed
        if t < frames - 1:
            mixed = mixed + taps_ref[2:3, :] * z_ref[t + 1]
        power = jnp.mean(mixed * mixed, axis=-1, keepdims=True)
        normed = mixed * lax.rsqrt(power + 1e-06) * gain_ref[...]
        hidden.append(jax.nn.gelu(normed).astype(BF16))
    delta = lax.dot_general(
        mix_out_ref[...],
        jnp.concatenate(hidden, axis=0),
        (((1,), (1,)), ((), ())),
        preferred_element_type=F32,
    )
    count = mix_out_ref.shape[0]
    result = delta + place[:count]
    for t in range(frames):
        out_ref[:, t, :] = result[:, t * rows : (t + 1) * rows]


def peer(order, here, m, count):
    if order == "xor":
        return here ^ abs(m)
    if isinstance(here, int):
        return (here + m) % count
    return lax.rem(here + m + count, count)


def in_vmem(x):
    return pltpu.with_memory_space_constraint(x, pltpu.MemorySpace.VMEM)


def on_device(
    feature_maps,
    query_frame,
    query_row,
    query_col,
    track_order,
    conv_weight,
    conv_bias,
    head_weight,
    mix_in,
    temporal_taps,
    mix_gain,
    mix_out,
):
    frame_count = lax.axis_size("frame")
    track_count = lax.axis_size("track")
    frame_here = lax.axis_index("frame").astype(jnp.int32)
    track_here = lax.axis_index("track").astype(jnp.int32)
    f_dev, pixels, chan = feature_maps.shape
    total = track_order.shape[0]
    tr_dev = total // track_count
    sub_rows = tr_dev // frame_count
    hid = conv_weight.shape[0]
    mixw = mix_in.shape[1]
    maps = feature_maps.reshape(f_dev * pixels, chan)

    order = "xor" if frame_count & (frame_count - 1) == 0 else "ring"

    def send(x, m):
        pairs = [(i, peer(order, i, m, frame_count)) for i in range(frame_count)]
        return lax.ppermute(x, "frame", pairs)

    limits = pltpu.CompilerParams(vmem_limit_bytes=24 << 20)
    place = jnp.stack([frame_here, track_here])
    picks, held = pl.pallas_call(
        functools.partial(pick_kernel, frame_count, track_count),
        name="pick",
        out_shape=(pltpu.VMEM((tr_dev, chan), BF16), pltpu.VMEM((pixels, chan), BF16)),
        in_specs=[SMEM_SPEC] + [VMEM_SPEC] * 4 + [pl.BlockSpec(memory_space=pl.ANY)],
        out_specs=(VMEM_SPEC, VMEM_SPEC),
        scratch_shapes=[pltpu.SemaphoreType.DMA((4,))],
        compiler_params=limits,
    )(
        place,
        track_order.reshape(1, total),
        query_frame.reshape(1, total),
        query_row.reshape(1, total),
        query_col.reshape(1, total),
        maps,
    )
    queries = [picks] + [send(picks, m) for m in range(1, frame_count)]

    part = 2 * TILE
    weight = pl.pallas_call(
        prep_kernel,
        name="prep",
        out_shape=pltpu.VMEM((2, hid * part, KDIM), BF16),
        in_specs=[SMEM_SPEC],
        out_specs=VMEM_SPEC,
        compiler_params=limits,
    )(conv_weight)

    padded = ROWS_PAD * GRID_W
    pieces = pl.pallas_call(
        functools.partial(heat_kernel, frame_count, order),
        name="heat",
        out_shape=tuple(
            pltpu.VMEM((sub_rows, chan + LANES), BF16) for _ in range(frame_count)
        ),
        in_specs=[SMEM_SPEC] * 3 + [VMEM_SPEC] * (frame_count + 2),
        out_specs=tuple(VMEM_SPEC for _ in range(frame_count)),
        scratch_shapes=[
            pltpu.VMEM((padded, tr_dev), F32),
            pltpu.VMEM((padded, tr_dev), BF16),
            pltpu.VMEM((padded, tr_dev), BF16),
            pltpu.VMEM((GRID_W // TILE, TILE, tr_dev), BF16),
            pltpu.VMEM((GRID_W // TILE, TILE, tr_dev), BF16),
            pltpu.VMEM((pixels, tr_dev), F32),
            pltpu.VMEM((frame_count, sub_rows, chan + LANES), BF16),
        ],
        compiler_params=limits,
    )(
        frame_here.reshape(1),
        conv_bias,
        head_weight,
        *[in_vmem(q) for q in queries],
        in_vmem(held),
        in_vmem(weight),
    )
    got = [pieces[0]] + [send(pieces[m], m) for m in range(1, frame_count)]
    mixed = pl.pallas_call(
        functools.partial(mix_kernel, order, frame_count),
        name="mix",
        out_shape=jax.ShapeDtypeStruct((mix_out.shape[1], frame_count, sub_rows), F32),
        in_specs=[SMEM_SPEC] + [VMEM_SPEC] * (frame_count + 4),
        out_specs=VMEM_SPEC,
        scratch_shapes=[
            pltpu.VMEM((frame_count, sub_rows, mixw), F32),
            pltpu.VMEM((frame_count, sub_rows, LANES), BF16),
        ],
        compiler_params=limits,
    )(
        frame_here.reshape(1),
        *[in_vmem(g) for g in got],
        in_vmem(mix_in),
        in_vmem(temporal_taps),
        in_vmem(mix_gain.reshape(1, mixw)),
        in_vmem(mix_out.T),
    )
    return jnp.transpose(mixed, (2, 0, 1))


def solution(mesh):
    placed = (
        P(("clip", "frame"), None, None),
        P("clip"),
        P("clip"),
        P("clip"),
        P("clip"),
        P(),
        P(),
        P(),
        P(),
        P(),
        P(),
        P(),
    )
    return jax.shard_map(
        on_device,
        mesh=mesh,
        in_specs=placed,
        out_specs=P(("clip", "frame", "track"), None, None),
        check_vma=False,
    )
```

```python
import functools
import math

import jax
import jax.numpy as jnp
from jax import lax
from jax.experimental import pallas as pl
from jax.experimental.pallas import tpu as pltpu
from jax.sharding import PartitionSpec as P

GRID_H = 64
GRID_W = 64
TILE = 16
KDIM = 256
ROWS_PAD = GRID_H + 4
LANES = 128

VMEM_SPEC = pl.BlockSpec(memory_space=pltpu.VMEM)
SMEM_SPEC = pl.BlockSpec(memory_space=pltpu.SMEM)
F32 = jnp.float32
BF16 = jnp.bfloat16


def iota(shape, dim):
    return lax.broadcasted_iota(jnp.int32, shape, dim)


def pick_kernel(
    frame_count,
    track_count,
    order_hbm,
    qf_hbm,
    qr_hbm,
    qc_hbm,
    maps_hbm,
    out_ref,
    held_ref,
    index_ref,
    index_sem,
    sem,
):
    total = order_hbm.shape[1]
    slots = out_ref.shape[0]
    pixels, chan = held_ref.shape
    chunks = sem.shape[0]
    step = pixels // chunks
    small = [
        pltpu.make_async_copy(src, index_ref.at[n], index_sem.at[n])
        for n, src in enumerate((order_hbm, qf_hbm, qr_hbm, qc_hbm))
    ]
    copies = [
        pltpu.make_async_copy(
            maps_hbm.at[pl.ds(n * step, step)], held_ref.at[pl.ds(n * step, step)], sem.at[n]
        )
        for n in range(chunks)
    ]
    for copy in small + copies:
        copy.start()
    frame_here = lax.axis_index("frame").astype(jnp.int32)
    track_here = lax.axis_index("track").astype(jnp.int32)
    sub = slots // frame_count
    at = iota((1, slots), 1)
    slot = (at // sub * track_count + track_here) * sub + at % sub
    row = iota((total, slots), 0)
    hot = jnp.where(row == slot, 1.0, 0.0).astype(BF16)
    for copy in small:
        copy.wait()
    order = index_ref[0]
    blank = jnp.zeros((5, total), jnp.int32)
    table = jnp.concatenate([order // 256, order % 256, blank, blank[:1]], axis=0)
    found = jnp.dot(table.astype(F32).astype(BF16), hot, preferred_element_type=F32)
    track = (found[0:1] * 256.0 + found[1:2]).astype(jnp.int32)
    hot = jnp.where(row == track, 1.0, 0.0).astype(BF16)
    table = jnp.concatenate([index_ref[1], index_ref[2], index_ref[3], blank], axis=0)
    found = jnp.dot(table.astype(F32).astype(BF16), hot, preferred_element_type=F32)
    flat = found[1:2] * GRID_W + found[2:3]
    flat = jnp.where(found[0:1] == frame_here.astype(F32), flat, -1.0)
    column = jnp.broadcast_to(flat, (slots, slots)).T[:, 0:1].astype(jnp.int32)
    acc = jnp.zeros((slots, chan), F32)
    for n in range(chunks):
        sel = jnp.where(iota((slots, step), 1) + n * step == column, 1.0, 0.0).astype(BF16)
        copies[n].wait()
        acc = acc + jnp.dot(
            sel, held_ref[n * step : (n + 1) * step, :], preferred_element_type=F32
        )
    out_ref[...] = acc.astype(BF16)


def prep_kernel(weight_ref, bias_ref, head_ref, out_ref, coef_ref):
    hid = weight_ref.shape[0]
    part = 2 * TILE
    row = iota((part, KDIM), 0)
    kk = iota((part, KDIM), 1)
    row_out, col_out = row // TILE, row % TILE
    mid = kk < 12 * TILE
    within = kk % (4 * TILE)
    seg = kk // (4 * TILE)
    edge = kk - 12 * TILE
    edge_seg = edge // TILE
    edge_at = edge % TILE
    use_low = jnp.where(mid, seg, edge_seg) == 2
    for parity in range(2):
        row_in = jnp.where(mid, within // TILE, edge_at % 8 - 2 * parity)
        col_in = jnp.where(mid, within % TILE, jnp.where(edge_at < 8, -1, TILE))
        down, across = row_in - row_out, col_in - col_out + 1
        good = (row_in >= 0) & (row_in < 4) & (down >= 0) & (down < 3)
        good = good & (across >= 0) & (across < 3) & (mid | (edge_seg < 3))
        tap = jnp.where(good, down * 3 + across, -1)
        masks = [tap == t for t in range(9)]
        for h in range(hid):
            full = jnp.zeros((part, KDIM), F32)
            for t in range(9):
                full = jnp.where(masks[t], weight_ref[h, t], full)
            high = full.astype(BF16).astype(F32)
            value = jnp.where(use_low, full - high, high)
            out_ref[parity, h * part : (h + 1) * part, :] = value.astype(BF16)
    const = 0.0
    for h in range(hid):
        coef_ref[h] = jnp.full(coef_ref.shape[1:], -bias_ref[h], F32)
        coef_ref[hid + h] = jnp.full(coef_ref.shape[1:], head_ref[h], F32)
        const = const + head_ref[h] * bias_ref[h]
    coef_ref[2 * hid] = jnp.full(coef_ref.shape[1:], const, F32)


def heat_kernel(
    pieces,
    queries,
    order,
    *refs,
):
    q_refs = refs[:queries]
    maps_ref, weight_ref, coef_ref = refs[queries : queries + 3]
    rest = refs[queries + 3 :]
    out_refs = rest[:pieces]
    cost_ref, high_ref, low_ref, edge_high, edge_low, logit_ref, full_ref = rest[pieces:]
    pixels, chan = maps_ref.shape
    slots = q_refs[0].shape[0]
    hid = coef_ref.shape[0] // 2
    part = 2 * TILE
    here = lax.axis_index("frame").astype(jnp.int32)
    query = q_refs[0][...].astype(F32)
    for ref in q_refs[1:]:
        query = query + ref[...].astype(F32)
    turned_q = query.T.astype(BF16)
    scale = 1.0 / math.sqrt(chan)

    for lo, hi in ((0, GRID_W), (GRID_W + pixels, ROWS_PAD * GRID_W)):
        cost_ref[lo:hi, :] = jnp.zeros((hi - lo, slots), F32)
        high_ref[lo:hi, :] = jnp.zeros((hi - lo, slots), BF16)
        low_ref[lo:hi, :] = jnp.zeros((hi - lo, slots), BF16)

    step = 512

    def cost_step(n, carry):
        at = pl.multiple_of(n * step, step)
        cost = jnp.dot(maps_ref[pl.ds(at, step), :], turned_q, preferred_element_type=F32) * scale
        to = pl.multiple_of(at + GRID_W, GRID_W)
        high = cost.astype(BF16)
        cost_ref[pl.ds(to, step), :] = cost
        high_ref[pl.ds(to, step), :] = high
        low_ref[pl.ds(to, step), :] = (cost - high.astype(F32)).astype(BF16)
        return carry

    lax.fori_loop(0, pixels // step, cost_step, 0, unroll=4)

    cols = GRID_W // TILE
    def window_step(j, best):
        for k in range(cols):
            base = j * 4 * GRID_W + k * TILE
            left = (
                jnp.zeros((8, slots), F32)
                if k == 0
                else cost_ref[pl.ds(base - 1, 8, stride=GRID_W), :]
            )
            right = (
                jnp.zeros((8, slots), F32)
                if k == cols - 1
                else cost_ref[pl.ds(base + TILE, 8, stride=GRID_W), :]
            )
            both = jnp.concatenate([left, right], axis=0)
            high = both.astype(BF16)
            edge_high[k] = high
            edge_low[k] = (both - high.astype(F32)).astype(BF16)
        for parity in range(2):
            top = (4 * j + 2 * parity) * GRID_W
            for pair in range(cols // 2):
                sides = []
                for k in (2 * pair, 2 * pair + 1):
                    at = [pl.multiple_of(top + rr * GRID_W + k * TILE, TILE) for rr in range(4)]
                    mid_high = [high_ref[pl.ds(a, TILE), :] for a in at]
                    mid_low = [low_ref[pl.ds(a, TILE), :] for a in at]
                    eh, el = edge_high[k], edge_low[k]
                    sides.append(
                        jnp.concatenate(mid_high + mid_low + mid_high + [eh, el, eh, eh], axis=0)
                    )
                window = jnp.concatenate(sides, axis=1)
                act = jnp.dot(weight_ref[parity], window, preferred_element_type=F32)
                for side in range(2):
                    k = 2 * pair + side
                    lanes = slice(side * slots, (side + 1) * slots)
                    for q in range(part // 8):
                        acc = coef_ref[2 * hid]
                        for h in range(hid):
                            at = h * part + 8 * q
                            acc = acc + coef_ref[hid + h] * jnp.maximum(
                                act[at : at + 8, lanes], coef_ref[h]
                            )
                        to = top + (8 * q // TILE) * GRID_W + k * TILE + 8 * q % TILE
                        logit_ref[pl.ds(pl.multiple_of(to, 8), 8), :] = acc
                        best = jnp.maximum(best, acc)
        return best

    best = lax.fori_loop(0, GRID_H // 4, window_step, jnp.full((8, slots), -jnp.inf, F32), unroll=8)
    top_value = jnp.max(best, axis=0, keepdims=True)

    def exp_step(n, carry):
        row_acc, col_acc = carry
        for m in range(4):
            r = n * 4 + m
            at = pl.multiple_of(r * GRID_W, GRID_W)
            value = jnp.exp(logit_ref[pl.ds(at, GRID_W), :] - top_value)
            logit_ref[pl.ds(at, GRID_W), :] = value
            col_acc = col_acc + value
            parts = [value[8 * n : 8 * n + 8] for n in range(GRID_W // 8)]
            while len(parts) > 1:
                parts = [a + b for a, b in zip(parts[::2], parts[1::2])]
            row_acc = row_acc + parts[0] * (r.astype(F32) * (1.0 / (GRID_H - 1)))
        return row_acc, col_acc

    row_acc, col_acc = lax.fori_loop(
        0, GRID_H // 4, exp_step, (jnp.zeros((8, slots), F32), jnp.zeros((GRID_W, slots), F32)), unroll=4
    )
    total = jnp.sum(col_acc, axis=0, keepdims=True)
    inverse = 1.0 / total
    row_est = jnp.sum(row_acc, axis=0, keepdims=True) * inverse
    col_pos = iota((GRID_W, slots), 0).astype(F32) * (1.0 / (GRID_W - 1))
    col_est = jnp.sum(col_acc * col_pos, axis=0, keepdims=True) * inverse

    def sample_step(n, acc):
        at = pl.multiple_of(n * step, step)
        heat = (logit_ref[pl.ds(at, step), :] * inverse).astype(BF16)
        return acc + jnp.dot(heat.T, maps_ref[pl.ds(at, step), :], preferred_element_type=F32)

    sampled = lax.fori_loop(0, pixels // step, sample_step, jnp.zeros((slots, chan), F32), unroll=4)
    rest = jnp.concatenate([row_est, col_est, jnp.zeros((LANES - 2, slots), F32)], axis=0)
    sub = slots // pieces
    full_ref[:, :, :chan] = sampled.astype(BF16).reshape(pieces, sub, chan)
    full_ref[:, :, chan:] = rest.T.astype(BF16).reshape(pieces, sub, LANES)
    for m in range(pieces):
        out_refs[m][...] = full_ref[peer(order, here, m, pieces)]


def mix_kernel(order, frames, *refs):
    got_refs = refs[:frames]
    mix_in_ref, taps_ref, gain_ref, mix_out_ref, out_ref, z_ref, place_ref = refs[frames:]
    chan = mix_in_ref.shape[0]
    rows = got_refs[0].shape[0]
    here = lax.axis_index("frame").astype(jnp.int32)
    joined = jnp.concatenate([ref[...] for ref in got_refs], axis=0)
    z = jnp.dot(joined[:, :chan], mix_in_ref[...], preferred_element_type=F32)
    for m in range(frames):
        source = peer(order, here, -m, frames)
        z_ref[source] = z[m * rows : (m + 1) * rows]
        place_ref[source] = got_refs[m][:, chan:]
    place = place_ref[...].astype(F32).reshape(frames * rows, LANES).T[:8]
    hidden = []
    for t in range(frames):
        mixed = taps_ref[1:2, :] * z_ref[t]
        if t > 0:
            mixed = taps_ref[0:1, :] * z_ref[t - 1] + mixed
        if t < frames - 1:
            mixed = mixed + taps_ref[2:3, :] * z_ref[t + 1]
        power = jnp.mean(mixed * mixed, axis=-1, keepdims=True)
        normed = mixed * lax.rsqrt(power + 1e-06) * gain_ref[...]
        hidden.append(jax.nn.gelu(normed).astype(BF16))
    delta = lax.dot_general(
        mix_out_ref[...],
        jnp.concatenate(hidden, axis=0),
        (((1,), (1,)), ((), ())),
        preferred_element_type=F32,
    )
    count = mix_out_ref.shape[0]
    result = delta + place[:count]
    for t in range(frames):
        out_ref[:, t, :] = result[:, t * rows : (t + 1) * rows]


def peer(order, here, m, count):
    if order == "xor":
        return here ^ abs(m)
    if isinstance(here, int):
        return (here + m) % count
    return lax.rem(here + m + count, count)


def in_hbm(x):
    return pltpu.with_memory_space_constraint(x, pltpu.MemorySpace.HBM)


def in_vmem(x):
    return pltpu.with_memory_space_constraint(x, pltpu.MemorySpace.VMEM)


def on_device(
    feature_maps,
    query_frame,
    query_row,
    query_col,
    track_order,
    conv_weight,
    conv_bias,
    head_weight,
    mix_in,
    temporal_taps,
    mix_gain,
    mix_out,
):
    frame_count = lax.axis_size("frame")
    track_count = lax.axis_size("track")
    f_dev, pixels, chan = feature_maps.shape
    total = track_order.shape[0]
    tr_dev = total // track_count
    sub_rows = tr_dev // frame_count
    hid = conv_weight.shape[0]
    mixw = mix_in.shape[1]
    maps = feature_maps.reshape(f_dev * pixels, chan)

    order = "xor" if frame_count & (frame_count - 1) == 0 else "ring"

    def send(x, m):
        pairs = [(i, peer(order, i, m, frame_count)) for i in range(frame_count)]
        return lax.ppermute(x, "frame", pairs)

    limits = pltpu.CompilerParams(vmem_limit_bytes=24 << 20)
    any_spec = pl.BlockSpec(memory_space=pl.ANY)
    picks, held = pl.pallas_call(
        functools.partial(pick_kernel, frame_count, track_count),
        name="pick",
        out_shape=(pltpu.VMEM((tr_dev, chan), BF16), pltpu.VMEM((pixels, chan), BF16)),
        in_specs=[any_spec] * 5,
        out_specs=(VMEM_SPEC, VMEM_SPEC),
        scratch_shapes=[
            pltpu.VMEM((4, 1, total), jnp.int32),
            pltpu.SemaphoreType.DMA((4,)),
            pltpu.SemaphoreType.DMA((4,)),
        ],
        compiler_params=limits,
    )(
        in_hbm(track_order.reshape(1, total)),
        in_hbm(query_frame.reshape(1, total)),
        in_hbm(query_row.reshape(1, total)),
        in_hbm(query_col.reshape(1, total)),
        in_hbm(maps),
    )
    if order == "xor":
        queries, reach = [picks], 1
        while reach < frame_count:
            mine = queries[0] if len(queries) == 1 else queries[0] + queries[1]
            queries = [mine, send(mine, reach)]
            reach *= 2
    else:
        queries = [picks] + [send(picks, m) for m in range(1, frame_count)]

    part = 2 * TILE
    weight, coef = pl.pallas_call(
        prep_kernel,
        name="prep",
        out_shape=(
            pltpu.VMEM((2, hid * part, KDIM), BF16),
            pltpu.VMEM((2 * hid + 1, 8, tr_dev), F32),
        ),
        in_specs=[SMEM_SPEC] * 3,
        out_specs=(VMEM_SPEC, VMEM_SPEC),
        compiler_params=limits,
    )(conv_weight, conv_bias, head_weight)

    padded = ROWS_PAD * GRID_W
    pieces = pl.pallas_call(
        functools.partial(heat_kernel, frame_count, len(queries), order),
        name="heat",
        out_shape=tuple(
            pltpu.VMEM((sub_rows, chan + LANES), BF16) for _ in range(frame_count)
        ),
        in_specs=[VMEM_SPEC] * (len(queries) + 3),
        out_specs=tuple(VMEM_SPEC for _ in range(frame_count)),
        scratch_shapes=[
            pltpu.VMEM((padded, tr_dev), F32),
            pltpu.VMEM((padded, tr_dev), BF16),
            pltpu.VMEM((padded, tr_dev), BF16),
            pltpu.VMEM((GRID_W // TILE, TILE, tr_dev), BF16),
            pltpu.VMEM((GRID_W // TILE, TILE, tr_dev), BF16),
            pltpu.VMEM((pixels, tr_dev), F32),
            pltpu.VMEM((frame_count, sub_rows, chan + LANES), BF16),
        ],
        compiler_params=limits,
    )(
        *[in_vmem(q) for q in queries],
        in_vmem(held),
        in_vmem(weight),
        in_vmem(coef),
    )
    got = [pieces[0]] + [send(pieces[m], m) for m in range(1, frame_count)]
    mixed = pl.pallas_call(
        functools.partial(mix_kernel, order, frame_count),
        name="mix",
        out_shape=jax.ShapeDtypeStruct((mix_out.shape[1], frame_count, sub_rows), F32),
        in_specs=[VMEM_SPEC] * (frame_count + 4),
        out_specs=VMEM_SPEC,
        scratch_shapes=[
            pltpu.VMEM((frame_count, sub_rows, mixw), F32),
            pltpu.VMEM((frame_count, sub_rows, LANES), BF16),
        ],
        compiler_params=limits,
    )(
        *[in_vmem(g) for g in got],
        in_vmem(mix_in),
        in_vmem(temporal_taps),
        in_vmem(mix_gain.reshape(1, mixw)),
        in_vmem(mix_out.T),
    )
    return jnp.transpose(mixed, (2, 0, 1))


def solution(mesh):
    placed = (
        P(("clip", "frame"), None, None),
        P("clip"),
        P("clip"),
        P("clip"),
        P("clip"),
        P(),
        P(),
        P(),
        P(),
        P(),
        P(),
        P(),
    )
    return jax.shard_map(
        on_device,
        mesh=mesh,
        in_specs=placed,
        out_specs=P(("clip", "frame", "track"), None, None),
        check_vma=False,
    )
```

```python
import functools
import math

import jax
import jax.numpy as jnp
from jax import lax
from jax.experimental import pallas as pl
from jax.experimental.pallas import tpu as pltpu
from jax.sharding import PartitionSpec as P

GRID_H = 64
GRID_W = 64
TILE = 16
KDIM = 256
ROWS_PAD = GRID_H + 4
LANES = 128

VMEM_SPEC = pl.BlockSpec(memory_space=pltpu.VMEM)
SMEM_SPEC = pl.BlockSpec(memory_space=pltpu.SMEM)
F32 = jnp.float32
BF16 = jnp.bfloat16


def iota(shape, dim):
    return lax.broadcasted_iota(jnp.int32, shape, dim)


def pick_kernel(
    frame_count,
    track_count,
    order_hbm,
    qf_hbm,
    qr_hbm,
    qc_hbm,
    maps_hbm,
    out_ref,
    held_ref,
    index_ref,
    index_sem,
    sem,
):
    total = order_hbm.shape[1]
    slots = out_ref.shape[0]
    pixels, chan = held_ref.shape
    chunks = sem.shape[0]
    step = pixels // chunks
    small = [
        pltpu.make_async_copy(src, index_ref.at[n], index_sem.at[n])
        for n, src in enumerate((order_hbm, qf_hbm, qr_hbm, qc_hbm))
    ]
    copies = [
        pltpu.make_async_copy(
            maps_hbm.at[pl.ds(n * step, step)], held_ref.at[pl.ds(n * step, step)], sem.at[n]
        )
        for n in range(chunks)
    ]
    for copy in small + copies:
        copy.start()
    frame_here = lax.axis_index("frame").astype(jnp.int32)
    track_here = lax.axis_index("track").astype(jnp.int32)
    sub = slots // frame_count
    at = iota((1, slots), 1)
    slot = (at // sub * track_count + track_here) * sub + at % sub
    row = iota((total, slots), 0)
    hot = jnp.where(row == slot, 1.0, 0.0).astype(BF16)
    for copy in small:
        copy.wait()
    order = index_ref[0]
    blank = jnp.zeros((5, total), jnp.int32)
    table = jnp.concatenate([order // 256, order % 256, blank, blank[:1]], axis=0)
    found = jnp.dot(table.astype(F32).astype(BF16), hot, preferred_element_type=F32)
    track = (found[0:1] * 256.0 + found[1:2]).astype(jnp.int32)
    hot = jnp.where(row == track, 1.0, 0.0).astype(BF16)
    table = jnp.concatenate([index_ref[1], index_ref[2], index_ref[3], blank], axis=0)
    found = jnp.dot(table.astype(F32).astype(BF16), hot, preferred_element_type=F32)
    flat = found[1:2] * GRID_W + found[2:3]
    flat = jnp.where(found[0:1] == frame_here.astype(F32), flat, -1.0)
    column = jnp.broadcast_to(flat, (slots, slots)).T[:, 0:1].astype(jnp.int32)
    acc = jnp.zeros((slots, chan), F32)
    for n in range(chunks):
        sel = jnp.where(iota((slots, step), 1) + n * step == column, 1.0, 0.0).astype(BF16)
        copies[n].wait()
        acc = acc + jnp.dot(
            sel, held_ref[n * step : (n + 1) * step, :], preferred_element_type=F32
        )
    out_ref[...] = acc.astype(BF16)


def prep_kernel(weight_ref, bias_ref, head_ref, out_ref, coef_ref):
    hid = weight_ref.shape[0]
    part = 2 * TILE
    row = iota((part, KDIM), 0)
    kk = iota((part, KDIM), 1)
    row_out, col_out = row // TILE, row % TILE
    mid = kk < 12 * TILE
    within = kk % (4 * TILE)
    seg = kk // (4 * TILE)
    edge = kk - 12 * TILE
    edge_seg = edge // TILE
    edge_at = edge % TILE
    use_low = jnp.where(mid, seg, edge_seg) == 2
    for parity in range(2):
        row_in = jnp.where(mid, within // TILE, edge_at % 8 - 2 * parity)
        col_in = jnp.where(mid, within % TILE, jnp.where(edge_at < 8, -1, TILE))
        down, across = row_in - row_out, col_in - col_out + 1
        good = (row_in >= 0) & (row_in < 4) & (down >= 0) & (down < 3)
        good = good & (across >= 0) & (across < 3) & (mid | (edge_seg < 3))
        tap = jnp.where(good, down * 3 + across, -1)
        masks = [tap == t for t in range(9)]
        for h in range(hid):
            full = jnp.zeros((part, KDIM), F32)
            for t in range(9):
                full = jnp.where(masks[t], weight_ref[h, t], full)
            high = full.astype(BF16).astype(F32)
            value = jnp.where(use_low, full - high, high)
            out_ref[parity, h * part : (h + 1) * part, :] = value.astype(BF16)
    const = 0.0
    for h in range(hid):
        coef_ref[h] = jnp.full(coef_ref.shape[1:], -bias_ref[h], F32)
        coef_ref[hid + h] = jnp.full(coef_ref.shape[1:], head_ref[h], F32)
        const = const + head_ref[h] * bias_ref[h]
    coef_ref[2 * hid] = jnp.full(coef_ref.shape[1:], const, F32)


def heat_kernel(
    pieces,
    queries,
    *refs,
):
    q_refs = refs[:queries]
    maps_ref, weight_ref, coef_ref = refs[queries : queries + 3]
    rest = refs[queries + 3 :]
    out_refs = rest[:pieces]
    cost_ref, high_ref, low_ref, edge_high, edge_low, logit_ref, full_ref = rest[pieces:]
    pixels, chan = maps_ref.shape
    slots = q_refs[0].shape[0]
    hid = coef_ref.shape[0] // 2
    part = 2 * TILE
    here = lax.axis_index("frame").astype(jnp.int32)
    query = q_refs[0][...].astype(F32)
    for ref in q_refs[1:]:
        query = query + ref[...].astype(F32)
    turned_q = query.T.astype(BF16)
    scale = 1.0 / math.sqrt(chan)

    for lo, hi in ((0, GRID_W), (GRID_W + pixels, ROWS_PAD * GRID_W)):
        cost_ref[lo:hi, :] = jnp.zeros((hi - lo, slots), F32)
        high_ref[lo:hi, :] = jnp.zeros((hi - lo, slots), BF16)
        low_ref[lo:hi, :] = jnp.zeros((hi - lo, slots), BF16)

    step = 512

    def cost_step(n, carry):
        at = pl.multiple_of(n * step, step)
        cost = jnp.dot(maps_ref[pl.ds(at, step), :], turned_q, preferred_element_type=F32) * scale
        to = pl.multiple_of(at + GRID_W, GRID_W)
        high = cost.astype(BF16)
        cost_ref[pl.ds(to, step), :] = cost
        high_ref[pl.ds(to, step), :] = high
        low_ref[pl.ds(to, step), :] = (cost - high.astype(F32)).astype(BF16)
        return carry

    lax.fori_loop(0, pixels // step, cost_step, 0, unroll=4)

    cols = GRID_W // TILE
    def window_step(j, best):
        for k in range(cols):
            base = j * 4 * GRID_W + k * TILE
            left = (
                jnp.zeros((8, slots), F32)
                if k == 0
                else cost_ref[pl.ds(base - 1, 8, stride=GRID_W), :]
            )
            right = (
                jnp.zeros((8, slots), F32)
                if k == cols - 1
                else cost_ref[pl.ds(base + TILE, 8, stride=GRID_W), :]
            )
            both = jnp.concatenate([left, right], axis=0)
            high = both.astype(BF16)
            edge_high[k] = high
            edge_low[k] = (both - high.astype(F32)).astype(BF16)
        for parity in range(2):
            top = (4 * j + 2 * parity) * GRID_W
            for pair in range(cols // 2):
                sides = []
                for k in (2 * pair, 2 * pair + 1):
                    at = [pl.multiple_of(top + rr * GRID_W + k * TILE, TILE) for rr in range(4)]
                    mid_high = [high_ref[pl.ds(a, TILE), :] for a in at]
                    mid_low = [low_ref[pl.ds(a, TILE), :] for a in at]
                    eh, el = edge_high[k], edge_low[k]
                    sides.append(
                        jnp.concatenate(mid_high + mid_low + mid_high + [eh, el, eh, eh], axis=0)
                    )
                window = jnp.concatenate(sides, axis=1)
                act = jnp.dot(weight_ref[parity], window, preferred_element_type=F32)
                for side in range(2):
                    k = 2 * pair + side
                    lanes = slice(side * slots, (side + 1) * slots)
                    for q in range(part // 8):
                        acc = coef_ref[2 * hid]
                        for h in range(hid):
                            at = h * part + 8 * q
                            acc = acc + coef_ref[hid + h] * jnp.maximum(
                                act[at : at + 8, lanes], coef_ref[h]
                            )
                        to = top + (8 * q // TILE) * GRID_W + k * TILE + 8 * q % TILE
                        logit_ref[pl.ds(pl.multiple_of(to, 8), 8), :] = acc
                        best = jnp.maximum(best, acc)
        return best

    best = lax.fori_loop(0, GRID_H // 4, window_step, jnp.full((8, slots), -jnp.inf, F32), unroll=8)
    top_value = jnp.max(best, axis=0, keepdims=True)

    def exp_step(n, carry):
        row_acc, col_acc = carry
        for m in range(4):
            r = n * 4 + m
            at = pl.multiple_of(r * GRID_W, GRID_W)
            value = jnp.exp(logit_ref[pl.ds(at, GRID_W), :] - top_value)
            logit_ref[pl.ds(at, GRID_W), :] = value
            col_acc = col_acc + value
            parts = [value[8 * n : 8 * n + 8] for n in range(GRID_W // 8)]
            while len(parts) > 1:
                parts = [a + b for a, b in zip(parts[::2], parts[1::2])]
            row_acc = row_acc + parts[0] * (r.astype(F32) * (1.0 / (GRID_H - 1)))
        return row_acc, col_acc

    row_acc, col_acc = lax.fori_loop(
        0, GRID_H // 4, exp_step, (jnp.zeros((8, slots), F32), jnp.zeros((GRID_W, slots), F32)), unroll=4
    )
    total = jnp.sum(col_acc, axis=0, keepdims=True)
    inverse = 1.0 / total
    row_est = jnp.sum(row_acc, axis=0, keepdims=True) * inverse
    col_pos = iota((GRID_W, slots), 0).astype(F32) * (1.0 / (GRID_W - 1))
    col_est = jnp.sum(col_acc * col_pos, axis=0, keepdims=True) * inverse

    def sample_step(n, acc):
        at = pl.multiple_of(n * step, step)
        heat = (logit_ref[pl.ds(at, step), :] * inverse).astype(BF16)
        return acc + jnp.dot(heat.T, maps_ref[pl.ds(at, step), :], preferred_element_type=F32)

    sampled = lax.fori_loop(0, pixels // step, sample_step, jnp.zeros((slots, chan), F32), unroll=4)
    rest = jnp.concatenate([row_est, col_est, jnp.zeros((LANES - 2, slots), F32)], axis=0)
    sub = slots // pieces
    full_ref[:, :, :chan] = sampled.astype(BF16).reshape(pieces, sub, chan)
    full_ref[:, :, chan:] = rest.T.astype(BF16).reshape(pieces, sub, LANES)
    for m in range(pieces):
        out_refs[m][...] = full_ref[ahead(here, m, pieces)]


def mix_kernel(frames, *refs):
    got_refs = refs[:frames]
    mix_in_ref, taps_ref, gain_ref, mix_out_ref, out_ref, z_ref, place_ref = refs[frames:]
    chan = mix_in_ref.shape[0]
    rows = got_refs[0].shape[0]
    here = lax.axis_index("frame").astype(jnp.int32)
    joined = jnp.concatenate([ref[...] for ref in got_refs], axis=0)
    z = jnp.dot(joined[:, :chan], mix_in_ref[...], preferred_element_type=F32)
    for m in range(frames):
        source = ahead(here, -m, frames)
        z_ref[source] = z[m * rows : (m + 1) * rows]
        place_ref[source] = got_refs[m][:, chan:]
    place = place_ref[...].astype(F32).reshape(frames * rows, LANES).T[:8]
    hidden = []
    for t in range(frames):
        mixed = taps_ref[1:2, :] * z_ref[t]
        if t > 0:
            mixed = taps_ref[0:1, :] * z_ref[t - 1] + mixed
        if t < frames - 1:
            mixed = mixed + taps_ref[2:3, :] * z_ref[t + 1]
        power = jnp.mean(mixed * mixed, axis=-1, keepdims=True)
        normed = mixed * lax.rsqrt(power + 1e-06) * gain_ref[...]
        hidden.append(jax.nn.gelu(normed).astype(BF16))
    delta = lax.dot_general(
        mix_out_ref[...],
        jnp.concatenate(hidden, axis=0),
        (((1,), (1,)), ((), ())),
        preferred_element_type=F32,
    )
    count = mix_out_ref.shape[0]
    result = delta + place[:count]
    for t in range(frames):
        out_ref[:, t, :] = result[:, t * rows : (t + 1) * rows]


def ahead(here, m, count):
    if isinstance(here, int):
        return (here + m) % count
    return lax.rem(here + m + count, count)


def in_hbm(x):
    return pltpu.with_memory_space_constraint(x, pltpu.MemorySpace.HBM)


def in_vmem(x):
    return pltpu.with_memory_space_constraint(x, pltpu.MemorySpace.VMEM)


def on_device(
    feature_maps,
    query_frame,
    query_row,
    query_col,
    track_order,
    conv_weight,
    conv_bias,
    head_weight,
    mix_in,
    temporal_taps,
    mix_gain,
    mix_out,
):
    frame_count = lax.axis_size("frame")
    track_count = lax.axis_size("track")
    f_dev, pixels, chan = feature_maps.shape
    total = track_order.shape[0]
    tr_dev = total // track_count
    sub_rows = tr_dev // frame_count
    hid = conv_weight.shape[0]
    mixw = mix_in.shape[1]
    maps = feature_maps.reshape(f_dev * pixels, chan)

    def send(x, m):
        pairs = [(i, ahead(i, m, frame_count)) for i in range(frame_count)]
        return lax.ppermute(x, "frame", pairs)

    def swap(x, m):
        return lax.ppermute(x, "frame", [(i, i ^ m) for i in range(frame_count)])

    limits = pltpu.CompilerParams(vmem_limit_bytes=24 << 20)
    any_spec = pl.BlockSpec(memory_space=pl.ANY)
    picks, held = pl.pallas_call(
        functools.partial(pick_kernel, frame_count, track_count),
        name="pick",
        out_shape=(pltpu.VMEM((tr_dev, chan), BF16), pltpu.VMEM((pixels, chan), BF16)),
        in_specs=[any_spec] * 5,
        out_specs=(VMEM_SPEC, VMEM_SPEC),
        scratch_shapes=[
            pltpu.VMEM((4, 1, total), jnp.int32),
            pltpu.SemaphoreType.DMA((4,)),
            pltpu.SemaphoreType.DMA((4,)),
        ],
        compiler_params=limits,
    )(
        in_hbm(track_order.reshape(1, total)),
        in_hbm(query_frame.reshape(1, total)),
        in_hbm(query_row.reshape(1, total)),
        in_hbm(query_col.reshape(1, total)),
        in_hbm(maps),
    )
    if frame_count & (frame_count - 1) == 0:
        others = [1, *range(frame_count - 1, 1, -1)]
        queries = [picks] + [swap(picks, m) for m in others]
    else:
        queries = [picks] + [send(picks, m) for m in range(1, frame_count)]

    part = 2 * TILE
    weight, coef = pl.pallas_call(
        prep_kernel,
        name="prep",
        out_shape=(
            pltpu.VMEM((2, hid * part, KDIM), BF16),
            pltpu.VMEM((2 * hid + 1, 8, tr_dev), F32),
        ),
        in_specs=[SMEM_SPEC] * 3,
        out_specs=(VMEM_SPEC, VMEM_SPEC),
        compiler_params=limits,
    )(conv_weight, conv_bias, head_weight)

    padded = ROWS_PAD * GRID_W
    pieces = pl.pallas_call(
        functools.partial(heat_kernel, frame_count, len(queries)),
        name="heat",
        out_shape=tuple(
            pltpu.VMEM((sub_rows, chan + LANES), BF16) for _ in range(frame_count)
        ),
        in_specs=[VMEM_SPEC] * (len(queries) + 3),
        out_specs=tuple(VMEM_SPEC for _ in range(frame_count)),
        scratch_shapes=[
            pltpu.VMEM((padded, tr_dev), F32),
            pltpu.VMEM((padded, tr_dev), BF16),
            pltpu.VMEM((padded, tr_dev), BF16),
            pltpu.VMEM((GRID_W // TILE, TILE, tr_dev), BF16),
            pltpu.VMEM((GRID_W // TILE, TILE, tr_dev), BF16),
            pltpu.VMEM((pixels, tr_dev), F32),
            pltpu.VMEM((frame_count, sub_rows, chan + LANES), BF16),
        ],
        compiler_params=limits,
    )(
        *[in_vmem(q) for q in queries],
        in_vmem(held),
        in_vmem(weight),
        in_vmem(coef),
    )
    got = [pieces[0]] + [send(pieces[m], m) for m in range(1, frame_count)]
    mixed = pl.pallas_call(
        functools.partial(mix_kernel, frame_count),
        name="mix",
        out_shape=jax.ShapeDtypeStruct((mix_out.shape[1], frame_count, sub_rows), F32),
        in_specs=[VMEM_SPEC] * (frame_count + 4),
        out_specs=VMEM_SPEC,
        scratch_shapes=[
            pltpu.VMEM((frame_count, sub_rows, mixw), F32),
            pltpu.VMEM((frame_count, sub_rows, LANES), BF16),
        ],
        compiler_params=limits,
    )(
        *[in_vmem(g) for g in got],
        in_vmem(mix_in),
        in_vmem(temporal_taps),
        in_vmem(mix_gain.reshape(1, mixw)),
        in_vmem(mix_out.T),
    )
    return jnp.transpose(mixed, (2, 0, 1))


def solution(mesh):
    placed = (
        P(("clip", "frame"), None, None),
        P("clip"),
        P("clip"),
        P("clip"),
        P("clip"),
        P(),
        P(),
        P(),
        P(),
        P(),
        P(),
        P(),
    )
    return jax.shard_map(
        on_device,
        mesh=mesh,
        in_specs=placed,
        out_specs=P(("clip", "frame", "track"), None, None),
        check_vma=False,
    )
```

```python
import functools
import math

import jax
import jax.numpy as jnp
from jax import lax
from jax.experimental import pallas as pl
from jax.experimental.pallas import tpu as pltpu
from jax.sharding import PartitionSpec as P

GRID_H = 64
GRID_W = 64
TILE = 16
KDIM = 256
ROWS_PAD = GRID_H + 4
LANES = 128
CHUNK = 8
LOG2E = math.log2(math.e)

VMEM_SPEC = pl.BlockSpec(memory_space=pltpu.VMEM)
SMEM_SPEC = pl.BlockSpec(memory_space=pltpu.SMEM)
F32 = jnp.float32
BF16 = jnp.bfloat16


def iota(shape, dim):
    return lax.broadcasted_iota(jnp.int32, shape, dim)


def pick_kernel(
    frame_count,
    track_count,
    order_hbm,
    qf_hbm,
    qr_hbm,
    qc_hbm,
    maps_hbm,
    out_ref,
    held_ref,
    index_ref,
    index_sem,
    sem,
):
    total = order_hbm.shape[1]
    slots = out_ref.shape[0]
    pixels, chan = held_ref.shape
    chunks = sem.shape[0]
    step = pixels // chunks
    small = [
        pltpu.make_async_copy(src, index_ref.at[n], index_sem.at[n])
        for n, src in enumerate((order_hbm, qf_hbm, qr_hbm, qc_hbm))
    ]
    copies = [
        pltpu.make_async_copy(
            maps_hbm.at[pl.ds(n * step, step)], held_ref.at[pl.ds(n * step, step)], sem.at[n]
        )
        for n in range(chunks)
    ]
    for copy in small + copies:
        copy.start()
    frame_here = lax.axis_index("frame").astype(jnp.int32)
    track_here = lax.axis_index("track").astype(jnp.int32)
    sub = slots // frame_count
    at = iota((1, slots), 1)
    slot = (at // sub * track_count + track_here) * sub + at % sub
    row = iota((total, slots), 0)
    hot = jnp.where(row == slot, 1.0, 0.0).astype(BF16)
    for copy in small:
        copy.wait()
    order = index_ref[0]
    blank = jnp.zeros((5, total), jnp.int32)
    table = jnp.concatenate([order // 256, order % 256, blank, blank[:1]], axis=0)
    found = jnp.dot(table.astype(F32).astype(BF16), hot, preferred_element_type=F32)
    track = (found[0:1] * 256.0 + found[1:2]).astype(jnp.int32)
    hot = jnp.where(row == track, 1.0, 0.0).astype(BF16)
    table = jnp.concatenate([index_ref[1], index_ref[2], index_ref[3], blank], axis=0)
    found = jnp.dot(table.astype(F32).astype(BF16), hot, preferred_element_type=F32)
    flat = found[1:2] * GRID_W + found[2:3]
    flat = jnp.where(found[0:1] == frame_here.astype(F32), flat, -1.0)
    column = jnp.broadcast_to(flat, (slots, slots)).T[:, 0:1].astype(jnp.int32)
    spread = jnp.broadcast_to(column, (slots, step))
    lane = iota((slots, step), 1)
    sums = [jnp.zeros((slots, chan), F32)] * 2
    for n in range(chunks):
        sel = jnp.where(spread == lane + n * step, 1.0, 0.0).astype(BF16)
        copies[n].wait()
        sums[n % 2] = sums[n % 2] + jnp.dot(
            sel, held_ref[n * step : (n + 1) * step, :], preferred_element_type=F32
        )
    out_ref[...] = (sums[0] + sums[1]).astype(BF16)


def prep_kernel(weight_ref, bias_ref, head_ref, out_ref, coef_ref):
    hid = weight_ref.shape[0]
    part = 2 * TILE
    row = iota((part, KDIM), 0)
    kk = iota((part, KDIM), 1)
    row_out, col_out = row // TILE, row % TILE
    mid = kk < 12 * TILE
    within = kk % (4 * TILE)
    seg = kk // (4 * TILE)
    edge = kk - 12 * TILE
    edge_seg = edge // TILE
    edge_at = edge % TILE
    use_low = jnp.where(mid, seg, edge_seg) == 2
    for parity in range(2):
        row_in = jnp.where(mid, within // TILE, edge_at % 8 - 2 * parity)
        col_in = jnp.where(mid, within % TILE, jnp.where(edge_at < 8, -1, TILE))
        down, across = row_in - row_out, col_in - col_out + 1
        good = (row_in >= 0) & (row_in < 4) & (down >= 0) & (down < 3)
        good = good & (across >= 0) & (across < 3) & (mid | (edge_seg < 3))
        tap = jnp.where(good, down * 3 + across, -1)
        masks = [tap == t for t in range(9)]
        for h in range(hid):
            full = jnp.zeros((part, KDIM), F32)
            for t in range(9):
                full = jnp.where(masks[t], weight_ref[h, t], full)
            high = full.astype(BF16).astype(F32)
            value = jnp.where(use_low, full - high, high)
            out_ref[parity, h * part : (h + 1) * part, :] = value.astype(BF16)
    const = 0.0
    for h in range(hid):
        coef_ref[h] = jnp.full(coef_ref.shape[1:], -bias_ref[h], F32)
        coef_ref[hid + h] = jnp.full(coef_ref.shape[1:], head_ref[h] * LOG2E, F32)
        const = const + head_ref[h] * bias_ref[h]
    coef_ref[2 * hid] = jnp.full(coef_ref.shape[1:], const * LOG2E, F32)


def heat_kernel(
    pieces,
    queries,
    *refs,
):
    q_refs = refs[:queries]
    maps_ref, weight_ref, coef_ref = refs[queries : queries + 3]
    rest = refs[queries + 3 :]
    out_refs = rest[:pieces]
    cost_ref, high_ref, low_ref, edge_high, edge_low, logit_ref, peak_ref, full_ref = rest[pieces:]
    pixels, chan = maps_ref.shape
    slots = q_refs[0].shape[0]
    hid = coef_ref.shape[0] // 2
    part = 2 * TILE
    here = lax.axis_index("frame").astype(jnp.int32)
    query = q_refs[0][...].astype(F32)
    for ref in q_refs[1:]:
        query = query + ref[...].astype(F32)
    turned_q = query.T.astype(BF16)
    scale = 1.0 / math.sqrt(chan)

    for lo, hi in ((0, GRID_W), (GRID_W + pixels, ROWS_PAD * GRID_W)):
        cost_ref[lo:hi, :] = jnp.zeros((hi - lo, slots), F32)
        high_ref[lo:hi, :] = jnp.zeros((hi - lo, slots), BF16)
        low_ref[lo:hi, :] = jnp.zeros((hi - lo, slots), BF16)

    step = 512

    def cost_step(n, carry):
        at = pl.multiple_of(n * step, step)
        cost = jnp.dot(maps_ref[pl.ds(at, step), :], turned_q, preferred_element_type=F32) * scale
        to = pl.multiple_of(at + GRID_W, GRID_W)
        high = cost.astype(BF16)
        cost_ref[pl.ds(to, step), :] = cost
        high_ref[pl.ds(to, step), :] = high
        low_ref[pl.ds(to, step), :] = (cost - high.astype(F32)).astype(BF16)
        return carry

    lax.fori_loop(0, pixels // step, cost_step, 0, unroll=8)

    cols = GRID_W // TILE
    def window_step(j, best):
        for k in range(cols):
            base = j * 4 * GRID_W + k * TILE
            left = (
                jnp.zeros((8, slots), F32)
                if k == 0
                else cost_ref[pl.ds(base - 1, 8, stride=GRID_W), :]
            )
            right = (
                jnp.zeros((8, slots), F32)
                if k == cols - 1
                else cost_ref[pl.ds(base + TILE, 8, stride=GRID_W), :]
            )
            both = jnp.concatenate([left, right], axis=0)
            high = both.astype(BF16)
            edge_high[k] = high
            edge_low[k] = (both - high.astype(F32)).astype(BF16)
        for parity in range(2):
            top = (4 * j + 2 * parity) * GRID_W
            for pair in range(cols // 2):
                sides = []
                for k in (2 * pair, 2 * pair + 1):
                    at = [pl.multiple_of(top + rr * GRID_W + k * TILE, TILE) for rr in range(4)]
                    mid_high = [high_ref[pl.ds(a, TILE), :] for a in at]
                    mid_low = [low_ref[pl.ds(a, TILE), :] for a in at]
                    eh, el = edge_high[k], edge_low[k]
                    sides.append(
                        jnp.concatenate(mid_high + mid_low + mid_high + [eh, el, eh, eh], axis=0)
                    )
                window = jnp.concatenate(sides, axis=1)
                act = jnp.dot(weight_ref[parity], window, preferred_element_type=F32)
                for side in range(2):
                    k = 2 * pair + side
                    lanes = slice(side * slots, (side + 1) * slots)
                    for q in range(part // 8):
                        acc = coef_ref[2 * hid]
                        for h in range(hid):
                            at = h * part + 8 * q
                            acc = acc + coef_ref[hid + h] * jnp.maximum(
                                act[at : at + 8, lanes], coef_ref[h]
                            )
                        to = top + (8 * q // TILE) * GRID_W + k * TILE + 8 * q % TILE
                        logit_ref[pl.ds(pl.multiple_of(to, 8), 8), :] = acc
                        best = jnp.maximum(best, acc)
        return best

    def chunk_step(c, carry):
        best, row_acc, col_acc = carry
        peak = best
        for m in range(CHUNK // 4):
            peak = window_step(c * (CHUNK // 4) + m, peak)
        peak_ref[c] = peak
        shrink = jnp.exp2(best - peak)
        row_acc = row_acc * shrink
        col_acc = [part * shrink for part in col_acc]
        for m in range(CHUNK):
            r = c * CHUNK + m
            values = []
            for n in range(GRID_W // 8):
                at = pl.multiple_of(r * GRID_W + 8 * n, 8)
                value = jnp.exp2(logit_ref[pl.ds(at, 8), :] - peak)
                logit_ref[pl.ds(at, 8), :] = value
                col_acc[n] = col_acc[n] + value
                values.append(value)
            while len(values) > 1:
                values = [x + y for x, y in zip(values[::2], values[1::2])]
            row_acc = row_acc + values[0] * (jnp.float32(r) * (1.0 / (GRID_H - 1)))
        return peak, row_acc, col_acc

    zero = jnp.zeros((8, slots), F32)
    best, row_acc, col_acc = lax.fori_loop(
        0,
        GRID_H // CHUNK,
        chunk_step,
        (jnp.full((8, slots), -jnp.inf, F32), zero, [zero] * (GRID_W // 8)),
        unroll=8,
    )
    top_value = jnp.max(best, axis=0, keepdims=True)
    shrink = jnp.exp2(best - top_value)
    total, col_sum = zero, zero
    for n in range(GRID_W // 8):
        col_pos = (iota((8, slots), 0) + 8 * n).astype(F32) * (1.0 / (GRID_W - 1))
        total = total + col_acc[n]
        col_sum = col_sum + col_acc[n] * col_pos
    inverse = 1.0 / jnp.sum(total * shrink, axis=0, keepdims=True)
    row_est = jnp.sum(row_acc * shrink, axis=0, keepdims=True) * inverse
    col_est = jnp.sum(col_sum * shrink, axis=0, keepdims=True) * inverse

    span = CHUNK * GRID_W

    def sample_step(c, acc):
        at = pl.multiple_of(c * span, span)
        factor = jnp.exp2(peak_ref[c] - top_value) * inverse
        heat = logit_ref[pl.ds(at, span), :].reshape(span // 8, 8, slots) * factor
        heat = heat.reshape(span, slots).astype(BF16)
        return acc + jnp.dot(heat.T, maps_ref[pl.ds(at, span), :], preferred_element_type=F32)

    sampled = lax.fori_loop(
        0, GRID_H // CHUNK, sample_step, jnp.zeros((slots, chan), F32), unroll=8
    )
    rest = jnp.concatenate([row_est, col_est, jnp.zeros((LANES - 2, slots), F32)], axis=0)
    sub = slots // pieces
    full_ref[:, :, :chan] = sampled.astype(BF16).reshape(pieces, sub, chan)
    full_ref[:, :, chan:] = rest.T.astype(BF16).reshape(pieces, sub, LANES)
    for m in range(pieces):
        out_refs[m][...] = full_ref[ahead(here, m, pieces)]


def mix_kernel(frames, *refs):
    got_refs = refs[:frames]
    mix_in_ref, taps_ref, gain_ref, mix_out_ref, out_ref, z_ref, place_ref = refs[frames:]
    chan = mix_in_ref.shape[0]
    rows = got_refs[0].shape[0]
    here = lax.axis_index("frame").astype(jnp.int32)
    joined = jnp.concatenate([ref[...] for ref in got_refs], axis=0)
    z = jnp.dot(joined[:, :chan], mix_in_ref[...], preferred_element_type=F32)
    for m in range(frames):
        source = ahead(here, -m, frames)
        z_ref[source] = z[m * rows : (m + 1) * rows]
        place_ref[source] = got_refs[m][:, chan:]
    place = place_ref[...].astype(F32).reshape(frames * rows, LANES).T[:8]
    hidden = []
    for t in range(frames):
        mixed = taps_ref[1:2, :] * z_ref[t]
        if t > 0:
            mixed = taps_ref[0:1, :] * z_ref[t - 1] + mixed
        if t < frames - 1:
            mixed = mixed + taps_ref[2:3, :] * z_ref[t + 1]
        power = jnp.mean(mixed * mixed, axis=-1, keepdims=True)
        normed = mixed * lax.rsqrt(power + 1e-06) * gain_ref[...]
        hidden.append(jax.nn.gelu(normed).astype(BF16))
    delta = lax.dot_general(
        mix_out_ref[...],
        jnp.concatenate(hidden, axis=0),
        (((1,), (1,)), ((), ())),
        preferred_element_type=F32,
    )
    count = mix_out_ref.shape[0]
    result = delta + place[:count]
    for t in range(frames):
        out_ref[:, t, :] = result[:, t * rows : (t + 1) * rows]


def ahead(here, m, count):
    if isinstance(here, int):
        return (here + m) % count
    return lax.rem(here + m + count, count)


def in_hbm(x):
    return pltpu.with_memory_space_constraint(x, pltpu.MemorySpace.HBM)


def in_vmem(x):
    return pltpu.with_memory_space_constraint(x, pltpu.MemorySpace.VMEM)


def on_device(
    feature_maps,
    query_frame,
    query_row,
    query_col,
    track_order,
    conv_weight,
    conv_bias,
    head_weight,
    mix_in,
    temporal_taps,
    mix_gain,
    mix_out,
):
    frame_count = lax.axis_size("frame")
    track_count = lax.axis_size("track")
    f_dev, pixels, chan = feature_maps.shape
    total = track_order.shape[0]
    tr_dev = total // track_count
    sub_rows = tr_dev // frame_count
    hid = conv_weight.shape[0]
    mixw = mix_in.shape[1]
    maps = feature_maps.reshape(f_dev * pixels, chan)

    def send(x, m):
        pairs = [(i, ahead(i, m, frame_count)) for i in range(frame_count)]
        return lax.ppermute(x, "frame", pairs)

    def swap(x, m):
        return lax.ppermute(x, "frame", [(i, i ^ m) for i in range(frame_count)])

    limits = pltpu.CompilerParams(vmem_limit_bytes=24 << 20)
    any_spec = pl.BlockSpec(memory_space=pl.ANY)
    picks, held = pl.pallas_call(
        functools.partial(pick_kernel, frame_count, track_count),
        name="pick",
        out_shape=(pltpu.VMEM((tr_dev, chan), BF16), pltpu.VMEM((pixels, chan), BF16)),
        in_specs=[any_spec] * 5,
        out_specs=(VMEM_SPEC, VMEM_SPEC),
        scratch_shapes=[
            pltpu.VMEM((4, 1, total), jnp.int32),
            pltpu.SemaphoreType.DMA((4,)),
            pltpu.SemaphoreType.DMA((2,)),
        ],
        compiler_params=limits,
    )(
        in_hbm(track_order.reshape(1, total)),
        in_hbm(query_frame.reshape(1, total)),
        in_hbm(query_row.reshape(1, total)),
        in_hbm(query_col.reshape(1, total)),
        in_hbm(maps),
    )
    if frame_count & (frame_count - 1) == 0:
        others = [1, *range(frame_count - 1, 1, -1)]
        queries = [picks] + [swap(picks, m) for m in others]
    else:
        queries = [picks] + [send(picks, m) for m in range(1, frame_count)]

    part = 2 * TILE
    weight, coef = pl.pallas_call(
        prep_kernel,
        name="prep",
        out_shape=(
            pltpu.VMEM((2, hid * part, KDIM), BF16),
            pltpu.VMEM((2 * hid + 1, 8, tr_dev), F32),
        ),
        in_specs=[SMEM_SPEC] * 3,
        out_specs=(VMEM_SPEC, VMEM_SPEC),
        compiler_params=limits,
    )(conv_weight, conv_bias, head_weight)

    padded = ROWS_PAD * GRID_W
    pieces = pl.pallas_call(
        functools.partial(heat_kernel, frame_count, len(queries)),
        name="heat",
        out_shape=tuple(
            pltpu.VMEM((sub_rows, chan + LANES), BF16) for _ in range(frame_count)
        ),
        in_specs=[VMEM_SPEC] * (len(queries) + 3),
        out_specs=tuple(VMEM_SPEC for _ in range(frame_count)),
        scratch_shapes=[
            pltpu.VMEM((padded, tr_dev), F32),
            pltpu.VMEM((padded, tr_dev), BF16),
            pltpu.VMEM((padded, tr_dev), BF16),
            pltpu.VMEM((GRID_W // TILE, TILE, tr_dev), BF16),
            pltpu.VMEM((GRID_W // TILE, TILE, tr_dev), BF16),
            pltpu.VMEM((pixels, tr_dev), F32),
            pltpu.VMEM((GRID_H // CHUNK, 8, tr_dev), F32),
            pltpu.VMEM((frame_count, sub_rows, chan + LANES), BF16),
        ],
        compiler_params=limits,
    )(
        *[in_vmem(q) for q in queries],
        in_vmem(held),
        in_vmem(weight),
        in_vmem(coef),
    )
    got = [pieces[0]] + [send(pieces[m], m) for m in range(1, frame_count)]
    mixed = pl.pallas_call(
        functools.partial(mix_kernel, frame_count),
        name="mix",
        out_shape=jax.ShapeDtypeStruct((mix_out.shape[1], frame_count, sub_rows), F32),
        in_specs=[VMEM_SPEC] * (frame_count + 4),
        out_specs=VMEM_SPEC,
        scratch_shapes=[
            pltpu.VMEM((frame_count, sub_rows, mixw), F32),
            pltpu.VMEM((frame_count, sub_rows, LANES), BF16),
        ],
        compiler_params=limits,
    )(
        *[in_vmem(g) for g in got],
        in_vmem(mix_in),
        in_vmem(temporal_taps),
        in_vmem(mix_gain.reshape(1, mixw)),
        in_vmem(mix_out.T),
    )
    return jnp.transpose(mixed, (2, 0, 1))


def solution(mesh):
    placed = (
        P(("clip", "frame"), None, None),
        P("clip"),
        P("clip"),
        P("clip"),
        P("clip"),
        P(),
        P(),
        P(),
        P(),
        P(),
        P(),
        P(),
    )
    return jax.shard_map(
        on_device,
        mesh=mesh,
        in_specs=placed,
        out_specs=P(("clip", "frame", "track"), None, None),
        check_vma=False,
    )
```

```python
import functools
import math

import jax
import jax.numpy as jnp
from jax import lax
from jax.experimental import pallas as pl
from jax.experimental.pallas import tpu as pltpu
from jax.sharding import PartitionSpec as P

GRID_H = 64
GRID_W = 64
TILE = 16
KDIM = 256
ROWS_PAD = GRID_H + 4
LANES = 128
CHUNK = 4
LOG2E = math.log2(math.e)

VMEM_SPEC = pl.BlockSpec(memory_space=pltpu.VMEM)
SMEM_SPEC = pl.BlockSpec(memory_space=pltpu.SMEM)
F32 = jnp.float32
BF16 = jnp.bfloat16


def iota(shape, dim):
    return lax.broadcasted_iota(jnp.int32, shape, dim)


def pick_kernel(
    frame_count,
    track_count,
    order_hbm,
    qf_hbm,
    qr_hbm,
    qc_hbm,
    maps_hbm,
    out_ref,
    held_ref,
    index_ref,
    index_sem,
    sem,
):
    total = order_hbm.shape[1]
    slots = out_ref.shape[0]
    pixels, chan = held_ref.shape
    chunks = sem.shape[0]
    step = pixels // chunks
    small = [
        pltpu.make_async_copy(src, index_ref.at[n], index_sem.at[n])
        for n, src in enumerate((order_hbm, qf_hbm, qr_hbm, qc_hbm))
    ]
    copies = [
        pltpu.make_async_copy(
            maps_hbm.at[pl.ds(n * step, step)], held_ref.at[pl.ds(n * step, step)], sem.at[n]
        )
        for n in range(chunks)
    ]
    for copy in small + copies:
        copy.start()
    frame_here = lax.axis_index("frame").astype(jnp.int32)
    track_here = lax.axis_index("track").astype(jnp.int32)
    sub = slots // frame_count
    at = iota((1, slots), 1)
    slot = (at // sub * track_count + track_here) * sub + at % sub
    row = iota((total, slots), 0)
    hot = jnp.where(row == slot, 1.0, 0.0).astype(BF16)
    for copy in small:
        copy.wait()
    order = index_ref[0]
    blank = jnp.zeros((5, total), jnp.int32)
    table = jnp.concatenate([order // 256, order % 256, blank, blank[:1]], axis=0)
    found = jnp.dot(table.astype(F32).astype(BF16), hot, preferred_element_type=F32)
    track = (found[0:1] * 256.0 + found[1:2]).astype(jnp.int32)
    hot = jnp.where(row == track, 1.0, 0.0).astype(BF16)
    table = jnp.concatenate([index_ref[1], index_ref[2], index_ref[3], blank], axis=0)
    found = jnp.dot(table.astype(F32).astype(BF16), hot, preferred_element_type=F32)
    flat = found[1:2] * GRID_W + found[2:3]
    flat = jnp.where(found[0:1] == frame_here.astype(F32), flat, -1.0)
    column = jnp.broadcast_to(flat, (slots, slots)).T[:, 0:1].astype(jnp.int32)
    spread = jnp.broadcast_to(column, (slots, step))
    lane = iota((slots, step), 1)
    sums = [jnp.zeros((slots, chan), F32)] * 2
    for n in range(chunks):
        sel = jnp.where(spread == lane + n * step, 1.0, 0.0).astype(BF16)
        copies[n].wait()
        sums[n % 2] = sums[n % 2] + jnp.dot(
            sel, held_ref[n * step : (n + 1) * step, :], preferred_element_type=F32
        )
    out_ref[...] = (sums[0] + sums[1]).astype(BF16)


def prep_kernel(weight_ref, bias_ref, head_ref, out_ref, coef_ref):
    hid = weight_ref.shape[0]
    part = 2 * TILE
    row = iota((part, KDIM), 0)
    kk = iota((part, KDIM), 1)
    row_out, col_out = row // TILE, row % TILE
    mid = kk < 12 * TILE
    within = kk % (4 * TILE)
    seg = kk // (4 * TILE)
    edge = kk - 12 * TILE
    edge_seg = edge // TILE
    edge_at = edge % TILE
    use_low = jnp.where(mid, seg, edge_seg) == 2
    for parity in range(2):
        row_in = jnp.where(mid, within // TILE, edge_at % 8 - 2 * parity)
        col_in = jnp.where(mid, within % TILE, jnp.where(edge_at < 8, -1, TILE))
        down, across = row_in - row_out, col_in - col_out + 1
        good = (row_in >= 0) & (row_in < 4) & (down >= 0) & (down < 3)
        good = good & (across >= 0) & (across < 3) & (mid | (edge_seg < 3))
        tap = jnp.where(good, down * 3 + across, -1)
        masks = [tap == t for t in range(9)]
        for h in range(hid):
            full = jnp.zeros((part, KDIM), F32)
            for t in range(9):
                full = jnp.where(masks[t], weight_ref[h, t], full)
            high = full.astype(BF16).astype(F32)
            value = jnp.where(use_low, full - high, high)
            out_ref[parity, h * part : (h + 1) * part, :] = value.astype(BF16)
    const = 0.0
    for h in range(hid):
        coef_ref[h] = jnp.full(coef_ref.shape[1:], -bias_ref[h], F32)
        coef_ref[hid + h] = jnp.full(coef_ref.shape[1:], head_ref[h] * LOG2E, F32)
        const = const + head_ref[h] * bias_ref[h]
    coef_ref[2 * hid] = jnp.full(coef_ref.shape[1:], const * LOG2E, F32)


def heat_kernel(
    pieces,
    queries,
    *refs,
):
    q_refs = refs[:queries]
    maps_ref, weight_ref, coef_ref = refs[queries : queries + 3]
    rest = refs[queries + 3 :]
    out_refs = rest[:pieces]
    cost_ref, high_ref, low_ref, edge_high, edge_low, logit_ref, peak_ref, full_ref = rest[pieces:]
    pixels, chan = maps_ref.shape
    slots = q_refs[0].shape[0]
    hid = coef_ref.shape[0] // 2
    part = 2 * TILE
    here = lax.axis_index("frame").astype(jnp.int32)
    query = q_refs[0][...].astype(F32)
    for ref in q_refs[1:]:
        query = query + ref[...].astype(F32)
    turned_q = query.T.astype(BF16)
    scale = 1.0 / math.sqrt(chan)

    for lo, hi in ((0, GRID_W), (GRID_W + pixels, ROWS_PAD * GRID_W)):
        cost_ref[lo:hi, :] = jnp.zeros((hi - lo, slots), F32)
        high_ref[lo:hi, :] = jnp.zeros((hi - lo, slots), BF16)
        low_ref[lo:hi, :] = jnp.zeros((hi - lo, slots), BF16)

    step = 512

    def cost_step(n, carry):
        at = pl.multiple_of(n * step, step)
        cost = jnp.dot(maps_ref[pl.ds(at, step), :], turned_q, preferred_element_type=F32) * scale
        to = pl.multiple_of(at + GRID_W, GRID_W)
        high = cost.astype(BF16)
        cost_ref[pl.ds(to, step), :] = cost
        high_ref[pl.ds(to, step), :] = high
        low_ref[pl.ds(to, step), :] = (cost - high.astype(F32)).astype(BF16)
        return carry

    lax.fori_loop(0, pixels // step, cost_step, 0, unroll=8)

    cols = GRID_W // TILE
    def window_step(j, best):
        for k in range(cols):
            base = j * 4 * GRID_W + k * TILE
            left = (
                jnp.zeros((8, slots), F32)
                if k == 0
                else cost_ref[pl.ds(base - 1, 8, stride=GRID_W), :]
            )
            right = (
                jnp.zeros((8, slots), F32)
                if k == cols - 1
                else cost_ref[pl.ds(base + TILE, 8, stride=GRID_W), :]
            )
            both = jnp.concatenate([left, right], axis=0)
            high = both.astype(BF16)
            edge_high[k] = high
            edge_low[k] = (both - high.astype(F32)).astype(BF16)
        for parity in range(2):
            top = (4 * j + 2 * parity) * GRID_W
            for pair in range(cols // 2):
                sides = []
                for k in (2 * pair, 2 * pair + 1):
                    at = [top + rr * GRID_W + k * TILE for rr in range(4)]
                    mid_high = [high_ref[pl.ds(a, TILE), :] for a in at]
                    mid_low = [low_ref[pl.ds(a, TILE), :] for a in at]
                    eh, el = edge_high[k], edge_low[k]
                    sides.append(
                        jnp.concatenate(mid_high + mid_low + mid_high + [eh, el, eh, eh], axis=0)
                    )
                window = jnp.concatenate(sides, axis=1)
                cuts = 2 if j == GRID_H // 4 - 1 and parity == 1 and pair >= 0 else 1
                length = hid * part // cuts
                act = jnp.concatenate(
                    [
                        jnp.dot(
                            weight_ref[parity, n * length : (n + 1) * length],
                            window,
                            preferred_element_type=F32,
                        )
                        for n in range(cuts)
                    ],
                    axis=0,
                )
                for side in range(2):
                    k = 2 * pair + side
                    lanes = slice(side * slots, (side + 1) * slots)
                    for q in range(part // 8):
                        acc = coef_ref[2 * hid]
                        for h in range(hid):
                            at = h * part + 8 * q
                            acc = acc + coef_ref[hid + h] * jnp.maximum(
                                act[at : at + 8, lanes], coef_ref[h]
                            )
                        to = top + (8 * q // TILE) * GRID_W + k * TILE + 8 * q % TILE
                        logit_ref[pl.ds(to, 8), :] = acc
                        best = jnp.maximum(best, acc)
        return best

    def chunk_step(c, carry):
        best, row_acc, col_acc = carry
        peak = best
        for m in range(CHUNK // 4):
            peak = window_step(c * (CHUNK // 4) + m, peak)
        peak_ref[c] = peak
        shrink = jnp.exp2(best - peak)
        row_acc = row_acc * shrink
        col_acc = [part * shrink for part in col_acc]
        for m in range(CHUNK):
            r = c * CHUNK + m
            values = []
            for n in range(GRID_W // 8):
                at = r * GRID_W + 8 * n
                value = jnp.exp2(logit_ref[pl.ds(at, 8), :] - peak)
                logit_ref[pl.ds(at, 8), :] = value
                col_acc[n] = col_acc[n] + value
                values.append(value)
            while len(values) > 1:
                values = [x + y for x, y in zip(values[::2], values[1::2])]
            row_acc = row_acc + values[0] * (r * (1.0 / (GRID_H - 1)))
        return peak, row_acc, col_acc

    zero = jnp.zeros((8, slots), F32)
    carry = (jnp.full((8, slots), -jnp.inf, F32), zero, [zero] * (GRID_W // 8))
    for c in range(GRID_H // CHUNK):
        carry = chunk_step(c, carry)
    best, row_acc, col_acc = carry
    top_value = jnp.max(best, axis=0, keepdims=True)
    shrink = jnp.exp2(best - top_value)
    total, col_sum = zero, zero
    for n in range(GRID_W // 8):
        col_pos = (iota((8, slots), 0) + 8 * n).astype(F32) * (1.0 / (GRID_W - 1))
        total = total + col_acc[n]
        col_sum = col_sum + col_acc[n] * col_pos
    inverse = 1.0 / jnp.sum(total * shrink, axis=0, keepdims=True)
    row_est = jnp.sum(row_acc * shrink, axis=0, keepdims=True) * inverse
    col_est = jnp.sum(col_sum * shrink, axis=0, keepdims=True) * inverse

    span = CHUNK * GRID_W

    each = GRID_H // CHUNK

    def sample_step(n, sums):
        sums = list(sums)
        for m in range(each):
            c = n * each + m
            at = pl.multiple_of(c * span, span)
            factor = jnp.exp2(peak_ref[c] - top_value) * inverse
            heat = logit_ref[pl.ds(at, span), :].reshape(span // 8, 8, slots) * factor
            heat = heat.reshape(span, slots).astype(BF16)
            sums[m % 2] = sums[m % 2] + jnp.dot(
                heat.T, maps_ref[pl.ds(at, span), :], preferred_element_type=F32
            )
        return tuple(sums)

    sums = lax.fori_loop(
        0, lax.min(here, 0) + 1, sample_step, (jnp.zeros((slots, chan), F32),) * 2
    )
    sampled = sums[0] + sums[1]
    rest = jnp.concatenate([row_est, col_est, jnp.zeros((LANES - 2, slots), F32)], axis=0)
    sub = slots // pieces
    full_ref[:, :, :chan] = sampled.astype(BF16).reshape(pieces, sub, chan)
    full_ref[:, :, chan:] = rest.T.astype(BF16).reshape(pieces, sub, LANES)
    for m in range(pieces):
        out_refs[m][...] = full_ref[ahead(here, m, pieces)]


def mix_kernel(frames, *refs):
    got_refs = refs[:frames]
    mix_in_ref, taps_ref, gain_ref, mix_out_ref, out_ref, z_ref, place_ref = refs[frames:]
    chan = mix_in_ref.shape[0]
    rows = got_refs[0].shape[0]
    here = lax.axis_index("frame").astype(jnp.int32)
    joined = jnp.concatenate([ref[...] for ref in got_refs], axis=0)
    z = jnp.dot(joined[:, :chan], mix_in_ref[...], preferred_element_type=F32)
    for m in range(frames):
        source = ahead(here, -m, frames)
        z_ref[source] = z[m * rows : (m + 1) * rows]
        place_ref[source] = got_refs[m][:, chan:]
    place = place_ref[...].astype(F32).reshape(frames * rows, LANES).T[:8]
    hidden = []
    for t in range(frames):
        mixed = taps_ref[1:2, :] * z_ref[t]
        if t > 0:
            mixed = taps_ref[0:1, :] * z_ref[t - 1] + mixed
        if t < frames - 1:
            mixed = mixed + taps_ref[2:3, :] * z_ref[t + 1]
        power = jnp.mean(mixed * mixed, axis=-1, keepdims=True)
        normed = mixed * lax.rsqrt(power + 1e-06) * gain_ref[...]
        hidden.append(jax.nn.gelu(normed).astype(BF16))
    delta = lax.dot_general(
        mix_out_ref[...],
        jnp.concatenate(hidden, axis=0),
        (((1,), (1,)), ((), ())),
        preferred_element_type=F32,
    )
    count = mix_out_ref.shape[0]
    result = delta + place[:count]
    for t in range(frames):
        out_ref[:, t, :] = result[:, t * rows : (t + 1) * rows]


def ahead(here, m, count):
    if isinstance(here, int):
        return (here + m) % count
    return lax.rem(here + m + count, count)


def in_hbm(x):
    return pltpu.with_memory_space_constraint(x, pltpu.MemorySpace.HBM)


def in_vmem(x):
    return pltpu.with_memory_space_constraint(x, pltpu.MemorySpace.VMEM)


def on_device(
    feature_maps,
    query_frame,
    query_row,
    query_col,
    track_order,
    conv_weight,
    conv_bias,
    head_weight,
    mix_in,
    temporal_taps,
    mix_gain,
    mix_out,
):
    frame_count = lax.axis_size("frame")
    track_count = lax.axis_size("track")
    f_dev, pixels, chan = feature_maps.shape
    total = track_order.shape[0]
    tr_dev = total // track_count
    sub_rows = tr_dev // frame_count
    hid = conv_weight.shape[0]
    mixw = mix_in.shape[1]
    maps = feature_maps.reshape(f_dev * pixels, chan)

    def send(x, m):
        pairs = [(i, ahead(i, m, frame_count)) for i in range(frame_count)]
        return lax.ppermute(x, "frame", pairs)

    def swap(x, m):
        return lax.ppermute(x, "frame", [(i, i ^ m) for i in range(frame_count)])

    limits = pltpu.CompilerParams(vmem_limit_bytes=24 << 20)
    any_spec = pl.BlockSpec(memory_space=pl.ANY)
    picks, held = pl.pallas_call(
        functools.partial(pick_kernel, frame_count, track_count),
        name="pick",
        out_shape=(pltpu.VMEM((tr_dev, chan), BF16), pltpu.VMEM((pixels, chan), BF16)),
        in_specs=[any_spec] * 5,
        out_specs=(VMEM_SPEC, VMEM_SPEC),
        scratch_shapes=[
            pltpu.VMEM((4, 1, total), jnp.int32),
            pltpu.SemaphoreType.DMA((4,)),
            pltpu.SemaphoreType.DMA((2,)),
        ],
        compiler_params=limits,
    )(
        in_hbm(track_order.reshape(1, total)),
        in_hbm(query_frame.reshape(1, total)),
        in_hbm(query_row.reshape(1, total)),
        in_hbm(query_col.reshape(1, total)),
        in_hbm(maps),
    )
    if frame_count & (frame_count - 1) == 0:
        others = [1, *range(frame_count - 1, 1, -1)]
        queries = [picks] + [swap(picks, m) for m in others]
    else:
        queries = [picks] + [send(picks, m) for m in range(1, frame_count)]

    part = 2 * TILE
    weight, coef = pl.pallas_call(
        prep_kernel,
        name="prep",
        out_shape=(
            pltpu.VMEM((2, hid * part, KDIM), BF16),
            pltpu.VMEM((2 * hid + 1, 8, tr_dev), F32),
        ),
        in_specs=[SMEM_SPEC] * 3,
        out_specs=(VMEM_SPEC, VMEM_SPEC),
        compiler_params=limits,
    )(conv_weight, conv_bias, head_weight)

    padded = ROWS_PAD * GRID_W
    pieces = pl.pallas_call(
        functools.partial(heat_kernel, frame_count, len(queries)),
        name="heat",
        out_shape=tuple(
            pltpu.VMEM((sub_rows, chan + LANES), BF16) for _ in range(frame_count)
        ),
        in_specs=[VMEM_SPEC] * (len(queries) + 3),
        out_specs=tuple(VMEM_SPEC for _ in range(frame_count)),
        scratch_shapes=[
            pltpu.VMEM((padded, tr_dev), F32),
            pltpu.VMEM((padded, tr_dev), BF16),
            pltpu.VMEM((padded, tr_dev), BF16),
            pltpu.VMEM((GRID_W // TILE, TILE, tr_dev), BF16),
            pltpu.VMEM((GRID_W // TILE, TILE, tr_dev), BF16),
            pltpu.VMEM((pixels, tr_dev), F32),
            pltpu.VMEM((GRID_H // CHUNK, 8, tr_dev), F32),
            pltpu.VMEM((frame_count, sub_rows, chan + LANES), BF16),
        ],
        compiler_params=limits,
    )(
        *[in_vmem(q) for q in queries],
        in_vmem(held),
        in_vmem(weight),
        in_vmem(coef),
    )
    got = [pieces[0]] + [send(pieces[m], m) for m in range(1, frame_count)]
    mixed = pl.pallas_call(
        functools.partial(mix_kernel, frame_count),
        name="mix",
        out_shape=jax.ShapeDtypeStruct((mix_out.shape[1], frame_count, sub_rows), F32),
        in_specs=[VMEM_SPEC] * (frame_count + 4),
        out_specs=VMEM_SPEC,
        scratch_shapes=[
            pltpu.VMEM((frame_count, sub_rows, mixw), F32),
            pltpu.VMEM((frame_count, sub_rows, LANES), BF16),
        ],
        compiler_params=limits,
    )(
        *[in_vmem(g) for g in got],
        in_vmem(mix_in),
        in_vmem(temporal_taps),
        in_vmem(mix_gain.reshape(1, mixw)),
        in_vmem(mix_out.T),
    )
    return jnp.transpose(mixed, (2, 0, 1))


def solution(mesh):
    placed = (
        P(("clip", "frame"), None, None),
        P("clip"),
        P("clip"),
        P("clip"),
        P("clip"),
        P(),
        P(),
        P(),
        P(),
        P(),
        P(),
        P(),
    )
    return jax.shard_map(
        on_device,
        mesh=mesh,
        in_specs=placed,
        out_specs=P(("clip", "frame", "track"), None, None),
        check_vma=False,
    )
```

```python
import functools
import math

import jax
import jax.numpy as jnp
from jax import lax
from jax.experimental import pallas as pl
from jax.experimental.pallas import tpu as pltpu
from jax.sharding import PartitionSpec as P

GRID_H = 64
GRID_W = 64
TILE = 16
KDIM = 256
ROWS_PAD = GRID_H + 4
LANES = 128
CHUNK = 4
LOG2E = math.log2(math.e)

VMEM_SPEC = pl.BlockSpec(memory_space=pltpu.VMEM)
SMEM_SPEC = pl.BlockSpec(memory_space=pltpu.SMEM)
F32 = jnp.float32
BF16 = jnp.bfloat16


def iota(shape, dim):
    return lax.broadcasted_iota(jnp.int32, shape, dim)


def pick_kernel(
    frame_count,
    track_count,
    order_hbm,
    qf_hbm,
    qr_hbm,
    qc_hbm,
    maps_hbm,
    out_ref,
    held_ref,
    index_ref,
    index_sem,
    sem,
):
    total = order_hbm.shape[1]
    slots = out_ref.shape[0]
    pixels, chan = held_ref.shape
    chunks = sem.shape[0]
    step = pixels // chunks
    small = [
        pltpu.make_async_copy(src, index_ref.at[n], index_sem.at[n])
        for n, src in enumerate((order_hbm, qf_hbm, qr_hbm, qc_hbm))
    ]
    copies = [
        pltpu.make_async_copy(
            maps_hbm.at[pl.ds(n * step, step)], held_ref.at[pl.ds(n * step, step)], sem.at[n]
        )
        for n in range(chunks)
    ]
    for copy in small + copies:
        copy.start()
    frame_here = lax.axis_index("frame").astype(jnp.int32)
    track_here = lax.axis_index("track").astype(jnp.int32)
    sub = slots // frame_count
    at = iota((1, slots), 1)
    slot = (at // sub * track_count + track_here) * sub + at % sub
    row = iota((total, slots), 0)
    hot = jnp.where(row == slot, 1.0, 0.0).astype(BF16)
    for copy in small:
        copy.wait()
    order = index_ref[0]
    blank = jnp.zeros((5, total), jnp.int32)
    table = jnp.concatenate([order // 256, order % 256, blank, blank[:1]], axis=0)
    found = jnp.dot(table.astype(F32).astype(BF16), hot, preferred_element_type=F32)
    track = (found[0:1] * 256.0 + found[1:2]).astype(jnp.int32)
    hot = jnp.where(row == track, 1.0, 0.0).astype(BF16)
    table = jnp.concatenate([index_ref[1], index_ref[2], index_ref[3], blank], axis=0)
    found = jnp.dot(table.astype(F32).astype(BF16), hot, preferred_element_type=F32)
    flat = found[1:2] * GRID_W + found[2:3]
    flat = jnp.where(found[0:1] == frame_here.astype(F32), flat, -1.0)
    column = jnp.broadcast_to(flat, (slots, slots)).T[:, 0:1].astype(jnp.int32)
    half = step // 2
    spread = jnp.broadcast_to(column, (slots, half))
    lane = iota((slots, half), 1)
    sums = [jnp.zeros((slots, chan), F32)] * 2
    for n in range(chunks):
        copies[n].wait()
        for m in range(2):
            at = n * step + m * half
            sel = jnp.where(spread == lane + at, 1.0, 0.0).astype(BF16)
            sums[m] = sums[m] + jnp.dot(
                sel, held_ref[at : at + half, :], preferred_element_type=F32
            )
    out_ref[...] = (sums[0] + sums[1]).astype(BF16)


def prep_kernel(weight_ref, bias_ref, head_ref, out_ref, coef_ref):
    hid = weight_ref.shape[0]
    part = 2 * TILE
    row = iota((part, KDIM), 0)
    kk = iota((part, KDIM), 1)
    row_out, col_out = row // TILE, row % TILE
    mid = kk < 12 * TILE
    within = kk % (4 * TILE)
    seg = kk // (4 * TILE)
    edge = kk - 12 * TILE
    edge_seg = edge // TILE
    edge_at = edge % TILE
    use_low = jnp.where(mid, seg, edge_seg) == 2
    for parity in range(2):
        row_in = jnp.where(mid, within // TILE, edge_at % 8 - 2 * parity)
        col_in = jnp.where(mid, within % TILE, jnp.where(edge_at < 8, -1, TILE))
        down, across = row_in - row_out, col_in - col_out + 1
        good = (row_in >= 0) & (row_in < 4) & (down >= 0) & (down < 3)
        good = good & (across >= 0) & (across < 3) & (mid | (edge_seg < 3))
        tap = jnp.where(good, down * 3 + across, -1)
        masks = [tap == t for t in range(9)]
        for h in range(hid):
            full = jnp.zeros((part, KDIM), F32)
            for t in range(9):
                full = jnp.where(masks[t], weight_ref[h, t], full)
            high = full.astype(BF16).astype(F32)
            value = jnp.where(use_low, full - high, high)
            out_ref[parity, h * part : (h + 1) * part, :] = value.astype(BF16)
    const = 0.0
    for h in range(hid):
        coef_ref[h] = jnp.full(coef_ref.shape[1:], -bias_ref[h], F32)
        coef_ref[hid + h] = jnp.full(coef_ref.shape[1:], head_ref[h] * LOG2E, F32)
        const = const + head_ref[h] * bias_ref[h]
    coef_ref[2 * hid] = jnp.full(coef_ref.shape[1:], const * LOG2E, F32)


def heat_kernel(
    pieces,
    queries,
    *refs,
):
    q_refs = refs[:queries]
    maps_ref, weight_ref, coef_ref = refs[queries : queries + 3]
    rest = refs[queries + 3 :]
    out_refs = rest[:pieces]
    cost_ref, high_ref, low_ref, edge_high, edge_low, logit_ref, peak_ref, full_ref = rest[pieces:]
    pixels, chan = maps_ref.shape
    slots = q_refs[0].shape[0]
    hid = coef_ref.shape[0] // 2
    part = 2 * TILE
    here = lax.axis_index("frame").astype(jnp.int32)
    query = q_refs[0][...]
    for ref in q_refs[1:]:
        query = query + ref[...]
    turned_q = query.T
    scale = 1.0 / math.sqrt(chan)

    for lo, hi in ((0, GRID_W), (GRID_W + pixels, ROWS_PAD * GRID_W)):
        cost_ref[lo:hi, :] = jnp.zeros((hi - lo, slots), F32)
        high_ref[lo:hi, :] = jnp.zeros((hi - lo, slots), BF16)
        low_ref[lo:hi, :] = jnp.zeros((hi - lo, slots), BF16)

    step = 512

    def cost_step(n, carry):
        at = pl.multiple_of(n * step, step)
        cost = jnp.dot(maps_ref[pl.ds(at, step), :], turned_q, preferred_element_type=F32) * scale
        to = pl.multiple_of(at + GRID_W, GRID_W)
        high = cost.astype(BF16)
        cost_ref[pl.ds(to, step), :] = cost
        high_ref[pl.ds(to, step), :] = high
        low_ref[pl.ds(to, step), :] = (cost - high.astype(F32)).astype(BF16)
        return carry

    lax.fori_loop(0, pixels // step, cost_step, 0, unroll=8)

    cols = GRID_W // TILE
    def window_step(j, best):
        for k in range(cols):
            base = j * 4 * GRID_W + k * TILE
            left = (
                jnp.zeros((8, slots), F32)
                if k == 0
                else cost_ref[pl.ds(base - 1, 8, stride=GRID_W), :]
            )
            right = (
                jnp.zeros((8, slots), F32)
                if k == cols - 1
                else cost_ref[pl.ds(base + TILE, 8, stride=GRID_W), :]
            )
            both = jnp.concatenate([left, right], axis=0)
            high = both.astype(BF16)
            edge_high[k] = high
            edge_low[k] = (both - high.astype(F32)).astype(BF16)
        for parity in range(2):
            top = (4 * j + 2 * parity) * GRID_W
            for pair in range(cols // 2):
                sides = []
                for k in (2 * pair, 2 * pair + 1):
                    at = [top + rr * GRID_W + k * TILE for rr in range(4)]
                    mid_high = [high_ref[pl.ds(a, TILE), :] for a in at]
                    mid_low = [low_ref[pl.ds(a, TILE), :] for a in at]
                    eh, el = edge_high[k], edge_low[k]
                    sides.append(
                        jnp.concatenate(mid_high + mid_low + mid_high + [eh, el, eh, eh], axis=0)
                    )
                window = jnp.concatenate(sides, axis=1)
                cuts = 2 if j == GRID_H // 4 - 1 and parity == 1 and pair >= 0 else 1
                length = hid * part // cuts
                act = jnp.concatenate(
                    [
                        jnp.dot(
                            weight_ref[parity, n * length : (n + 1) * length],
                            window,
                            preferred_element_type=F32,
                        )
                        for n in range(cuts)
                    ],
                    axis=0,
                )
                for side in range(2):
                    k = 2 * pair + side
                    lanes = slice(side * slots, (side + 1) * slots)
                    for q in range(part // 8):
                        acc = coef_ref[2 * hid]
                        for h in range(hid):
                            at = h * part + 8 * q
                            acc = acc + coef_ref[hid + h] * jnp.maximum(
                                act[at : at + 8, lanes], coef_ref[h]
                            )
                        to = top + (8 * q // TILE) * GRID_W + k * TILE + 8 * q % TILE
                        logit_ref[pl.ds(to, 8), :] = acc
                        best = jnp.maximum(best, acc)
        return best

    def chunk_step(c, carry):
        best, row_acc, col_acc = carry
        peak = best
        for m in range(CHUNK // 4):
            peak = window_step(c * (CHUNK // 4) + m, peak)
        peak_ref[c] = peak
        shrink = jnp.exp2(best - peak)
        row_acc = row_acc * shrink
        col_acc = [part * shrink for part in col_acc]
        for m in range(CHUNK):
            r = c * CHUNK + m
            values = []
            for n in range(GRID_W // 8):
                at = r * GRID_W + 8 * n
                value = jnp.exp2(logit_ref[pl.ds(at, 8), :] - peak)
                logit_ref[pl.ds(at, 8), :] = value
                col_acc[n] = col_acc[n] + value
                values.append(value)
            while len(values) > 1:
                values = [x + y for x, y in zip(values[::2], values[1::2])]
            row_acc = row_acc + values[0] * (r * (1.0 / (GRID_H - 1)))
        return peak, row_acc, col_acc

    zero = jnp.zeros((8, slots), F32)
    carry = (jnp.full((8, slots), -jnp.inf, F32), zero, [zero] * (GRID_W // 8))
    for c in range(GRID_H // CHUNK):
        carry = chunk_step(c, carry)
    best, row_acc, col_acc = carry
    top_value = jnp.max(best, axis=0, keepdims=True)
    shrink = jnp.exp2(best - top_value)
    total, col_sum = zero, zero
    for n in range(GRID_W // 8):
        col_pos = (iota((8, slots), 0) + 8 * n).astype(F32) * (1.0 / (GRID_W - 1))
        total = total + col_acc[n]
        col_sum = col_sum + col_acc[n] * col_pos
    inverse = 1.0 / jnp.sum(total * shrink, axis=0, keepdims=True)
    row_est = jnp.sum(row_acc * shrink, axis=0, keepdims=True) * inverse
    col_est = jnp.sum(col_sum * shrink, axis=0, keepdims=True) * inverse

    span = CHUNK * GRID_W

    each = GRID_H // CHUNK

    def sample_step(n, sums):
        sums = list(sums)
        for m in range(each):
            c = n * each + m
            at = pl.multiple_of(c * span, span)
            factor = jnp.exp2(peak_ref[c] - top_value) * inverse
            heat = logit_ref[pl.ds(at, span), :].reshape(span // 8, 8, slots) * factor
            heat = heat.reshape(span, slots).astype(BF16)
            sums[m % 2] = sums[m % 2] + jnp.dot(
                heat.T, maps_ref[pl.ds(at, span), :], preferred_element_type=F32
            )
        return tuple(sums)

    sums = lax.fori_loop(
        0, lax.min(here, 0) + 1, sample_step, (jnp.zeros((slots, chan), F32),) * 2
    )
    sampled = sums[0] + sums[1]
    rest = jnp.concatenate([row_est, col_est, jnp.zeros((LANES - 2, slots), F32)], axis=0)
    sub = slots // pieces
    full_ref[:, :, :chan] = sampled.astype(BF16).reshape(pieces, sub, chan)
    full_ref[:, :, chan:] = rest.T.astype(BF16).reshape(pieces, sub, LANES)
    for m in range(pieces):
        out_refs[m][...] = full_ref[ahead(here, m, pieces)]


def mix_kernel(frames, *refs):
    got_refs = refs[:frames]
    mix_in_ref, taps_ref, gain_ref, mix_out_ref, out_ref, z_ref, join_ref = refs[frames:]
    chan = mix_in_ref.shape[0]
    rows = got_refs[0].shape[0]
    here = lax.axis_index("frame").astype(jnp.int32)
    for m in range(frames):
        join_ref[ahead(here, -m, frames)] = got_refs[m][...]
    joined = join_ref[...].reshape(frames * rows, join_ref.shape[2])
    place = joined[:, chan:].astype(F32).T[:8]
    z_ref[...] = jnp.dot(
        joined[:, :chan], mix_in_ref[...], preferred_element_type=F32
    ).reshape(z_ref.shape)
    rate = math.sqrt(2.0 / math.pi)
    hidden = []
    for t in range(frames):
        mixed = taps_ref[1:2, :] * z_ref[t]
        if t > 0:
            mixed = taps_ref[0:1, :] * z_ref[t - 1] + mixed
        if t < frames - 1:
            mixed = mixed + taps_ref[2:3, :] * z_ref[t + 1]
        power = jnp.mean(mixed * mixed, axis=-1, keepdims=True)
        normed = mixed * lax.rsqrt(power + 1e-06) * gain_ref[...]
        curve = jnp.tanh(normed * (normed * normed * (0.044715 * rate) + rate))
        half = 0.5 * normed
        hidden.append((half * curve + half).astype(BF16))
    delta = lax.dot_general(
        mix_out_ref[...],
        jnp.concatenate(hidden, axis=0),
        (((1,), (1,)), ((), ())),
        preferred_element_type=F32,
    )
    count = mix_out_ref.shape[0]
    result = delta + place[:count]
    for t in range(frames):
        out_ref[:, t, :] = result[:, t * rows : (t + 1) * rows]


def ahead(here, m, count):
    if isinstance(here, int):
        return (here + m) % count
    return lax.rem(here + m + count, count)


def in_hbm(x):
    return pltpu.with_memory_space_constraint(x, pltpu.MemorySpace.HBM)


def in_vmem(x):
    return pltpu.with_memory_space_constraint(x, pltpu.MemorySpace.VMEM)


def on_device(
    feature_maps,
    query_frame,
    query_row,
    query_col,
    track_order,
    conv_weight,
    conv_bias,
    head_weight,
    mix_in,
    temporal_taps,
    mix_gain,
    mix_out,
):
    frame_count = lax.axis_size("frame")
    track_count = lax.axis_size("track")
    f_dev, pixels, chan = feature_maps.shape
    total = track_order.shape[0]
    tr_dev = total // track_count
    sub_rows = tr_dev // frame_count
    hid = conv_weight.shape[0]
    mixw = mix_in.shape[1]
    maps = feature_maps.reshape(f_dev * pixels, chan)

    def send(x, m):
        pairs = [(i, ahead(i, m, frame_count)) for i in range(frame_count)]
        return lax.ppermute(x, "frame", pairs)

    def swap(x, m):
        return lax.ppermute(x, "frame", [(i, i ^ m) for i in range(frame_count)])

    limits = pltpu.CompilerParams(vmem_limit_bytes=24 << 20)
    any_spec = pl.BlockSpec(memory_space=pl.ANY)
    picks, held = pl.pallas_call(
        functools.partial(pick_kernel, frame_count, track_count),
        name="pick",
        out_shape=(pltpu.VMEM((tr_dev, chan), BF16), pltpu.VMEM((pixels, chan), BF16)),
        in_specs=[any_spec] * 5,
        out_specs=(VMEM_SPEC, VMEM_SPEC),
        scratch_shapes=[
            pltpu.VMEM((4, 1, total), jnp.int32),
            pltpu.SemaphoreType.DMA((4,)),
            pltpu.SemaphoreType.DMA((2,)),
        ],
        compiler_params=limits,
    )(
        in_hbm(track_order.reshape(1, total)),
        in_hbm(query_frame.reshape(1, total)),
        in_hbm(query_row.reshape(1, total)),
        in_hbm(query_col.reshape(1, total)),
        in_hbm(maps),
    )
    if frame_count & (frame_count - 1) == 0:
        others = [1, *range(frame_count - 1, 1, -1)]
        queries = [picks] + [swap(picks, m) for m in others]
    else:
        queries = [picks] + [send(picks, m) for m in range(1, frame_count)]

    part = 2 * TILE
    weight, coef = pl.pallas_call(
        prep_kernel,
        name="prep",
        out_shape=(
            pltpu.VMEM((2, hid * part, KDIM), BF16),
            pltpu.VMEM((2 * hid + 1, 8, tr_dev), F32),
        ),
        in_specs=[SMEM_SPEC] * 3,
        out_specs=(VMEM_SPEC, VMEM_SPEC),
        compiler_params=limits,
    )(conv_weight, conv_bias, head_weight)

    padded = ROWS_PAD * GRID_W
    pieces = pl.pallas_call(
        functools.partial(heat_kernel, frame_count, len(queries)),
        name="heat",
        out_shape=tuple(
            pltpu.VMEM((sub_rows, chan + LANES), BF16) for _ in range(frame_count)
        ),
        in_specs=[VMEM_SPEC] * (len(queries) + 3),
        out_specs=tuple(VMEM_SPEC for _ in range(frame_count)),
        scratch_shapes=[
            pltpu.VMEM((padded, tr_dev), F32),
            pltpu.VMEM((padded, tr_dev), BF16),
            pltpu.VMEM((padded, tr_dev), BF16),
            pltpu.VMEM((GRID_W // TILE, TILE, tr_dev), BF16),
            pltpu.VMEM((GRID_W // TILE, TILE, tr_dev), BF16),
            pltpu.VMEM((pixels, tr_dev), F32),
            pltpu.VMEM((GRID_H // CHUNK, 8, tr_dev), F32),
            pltpu.VMEM((frame_count, sub_rows, chan + LANES), BF16),
        ],
        compiler_params=limits,
    )(
        *[in_vmem(q) for q in queries],
        in_vmem(held),
        in_vmem(weight),
        in_vmem(coef),
    )
    got = [pieces[0]] + [send(pieces[m], m) for m in range(1, frame_count)]
    mixed = pl.pallas_call(
        functools.partial(mix_kernel, frame_count),
        name="mix",
        out_shape=jax.ShapeDtypeStruct((mix_out.shape[1], frame_count, sub_rows), F32),
        in_specs=[VMEM_SPEC] * (frame_count + 4),
        out_specs=VMEM_SPEC,
        scratch_shapes=[
            pltpu.VMEM((frame_count, sub_rows, mixw), F32),
            pltpu.VMEM((frame_count, sub_rows, chan + LANES), BF16),
        ],
        compiler_params=limits,
    )(
        *[in_vmem(g) for g in got],
        in_vmem(mix_in),
        in_vmem(temporal_taps),
        in_vmem(mix_gain.reshape(1, mixw)),
        in_vmem(mix_out.T),
    )
    return jnp.transpose(mixed, (2, 0, 1))


def solution(mesh):
    placed = (
        P(("clip", "frame"), None, None),
        P("clip"),
        P("clip"),
        P("clip"),
        P("clip"),
        P(),
        P(),
        P(),
        P(),
        P(),
        P(),
        P(),
    )
    return jax.shard_map(
        on_device,
        mesh=mesh,
        in_specs=placed,
        out_specs=P(("clip", "frame", "track"), None, None),
        check_vma=False,
    )
```

```python
import functools
import math

import jax
import jax.numpy as jnp
from jax import lax
from jax.experimental import pallas as pl
from jax.experimental.pallas import tpu as pltpu
from jax.sharding import PartitionSpec as P

GRID_H = 64
GRID_W = 64
TILE = 16
KDIM = 256
ROWS_PAD = GRID_H + 4
LANES = 128
CHUNK = 4
LOG2E = math.log2(math.e)

VMEM_SPEC = pl.BlockSpec(memory_space=pltpu.VMEM)
SMEM_SPEC = pl.BlockSpec(memory_space=pltpu.SMEM)
F32 = jnp.float32
BF16 = jnp.bfloat16


def iota(shape, dim):
    return lax.broadcasted_iota(jnp.int32, shape, dim)


def pick_kernel(
    frame_count,
    track_count,
    order_hbm,
    qf_hbm,
    qr_hbm,
    qc_hbm,
    maps_hbm,
    out_ref,
    held_ref,
    index_ref,
    index_sem,
    sem,
):
    total = order_hbm.shape[1]
    slots = out_ref.shape[0]
    pixels, chan = held_ref.shape
    chunks = sem.shape[0]
    step = pixels // chunks
    small = [
        pltpu.make_async_copy(src, index_ref.at[n], index_sem.at[n])
        for n, src in enumerate((order_hbm, qf_hbm, qr_hbm, qc_hbm))
    ]
    copies = [
        pltpu.make_async_copy(
            maps_hbm.at[pl.ds(n * step, step)], held_ref.at[pl.ds(n * step, step)], sem.at[n]
        )
        for n in range(chunks)
    ]
    for copy in small + copies:
        copy.start()
    frame_here = lax.axis_index("frame").astype(jnp.int32)
    track_here = lax.axis_index("track").astype(jnp.int32)
    sub = slots // frame_count
    at = iota((1, slots), 1)
    slot = (at // sub * track_count + track_here) * sub + at % sub
    row = iota((total, slots), 0)
    hot = jnp.where(row == slot, 1.0, 0.0).astype(BF16)
    for copy in small:
        copy.wait()
    order = index_ref[0]
    blank = jnp.zeros((5, total), jnp.int32)
    table = jnp.concatenate([order // 256, order % 256, blank, blank[:1]], axis=0)
    found = jnp.dot(table.astype(F32).astype(BF16), hot, preferred_element_type=F32)
    track = (found[0:1] * 256.0 + found[1:2]).astype(jnp.int32)
    hot = jnp.where(row == track, 1.0, 0.0).astype(BF16)
    table = jnp.concatenate([index_ref[1], index_ref[2], index_ref[3], blank], axis=0)
    found = jnp.dot(table.astype(F32).astype(BF16), hot, preferred_element_type=F32)
    flat = found[1:2] * GRID_W + found[2:3]
    flat = jnp.where(found[0:1] == frame_here.astype(F32), flat, -1.0)
    column = jnp.broadcast_to(flat, (slots, slots)).T[:, 0:1].astype(jnp.int32)
    half = step // 2
    spread = jnp.broadcast_to(column, (slots, half))
    lane = iota((slots, half), 1)
    sums = [jnp.zeros((slots, chan), F32)] * 2
    for n in range(chunks):
        copies[n].wait()
        for m in range(2):
            at = n * step + m * half
            sel = jnp.where(spread == lane + at, 1.0, 0.0).astype(BF16)
            sums[m] = sums[m] + jnp.dot(
                sel, held_ref[at : at + half, :], preferred_element_type=F32
            )
    out_ref[...] = (sums[0] + sums[1]).astype(BF16)


def prep_kernel(weight_ref, bias_ref, head_ref, out_ref, coef_ref):
    hid = weight_ref.shape[0]
    part = 2 * TILE
    row = iota((part, KDIM), 0)
    kk = iota((part, KDIM), 1)
    row_out, col_out = row // TILE, row % TILE
    mid = kk < 12 * TILE
    within = kk % (4 * TILE)
    seg = kk // (4 * TILE)
    edge = kk - 12 * TILE
    edge_seg = edge // TILE
    edge_at = edge % TILE
    use_low = jnp.where(mid, seg, edge_seg) == 2
    for parity in range(2):
        row_in = jnp.where(mid, within // TILE, edge_at % 8 - 2 * parity)
        col_in = jnp.where(mid, within % TILE, jnp.where(edge_at < 8, -1, TILE))
        down, across = row_in - row_out, col_in - col_out + 1
        good = (row_in >= 0) & (row_in < 4) & (down >= 0) & (down < 3)
        good = good & (across >= 0) & (across < 3) & (mid | (edge_seg < 3))
        tap = jnp.where(good, down * 3 + across, -1)
        masks = [tap == t for t in range(9)]
        for h in range(hid):
            full = jnp.zeros((part, KDIM), F32)
            for t in range(9):
                full = jnp.where(masks[t], weight_ref[h, t], full)
            high = full.astype(BF16).astype(F32)
            value = jnp.where(use_low, full - high, high)
            out_ref[parity, h * part : (h + 1) * part, :] = value.astype(BF16)
    const = 0.0
    for h in range(hid):
        coef_ref[h] = jnp.full(coef_ref.shape[1:], -bias_ref[h], F32)
        coef_ref[hid + h] = jnp.full(coef_ref.shape[1:], head_ref[h] * LOG2E, F32)
        const = const + head_ref[h] * bias_ref[h]
    coef_ref[2 * hid] = jnp.full(coef_ref.shape[1:], const * LOG2E, F32)


def heat_kernel(
    pieces,
    queries,
    *refs,
):
    q_refs = refs[:queries]
    maps_ref, weight_ref, coef_ref = refs[queries : queries + 3]
    rest = refs[queries + 3 :]
    out_refs = rest[:pieces]
    cost_ref, high_ref, low_ref, edge_high, edge_low, logit_ref, peak_ref, full_ref = rest[pieces:]
    pixels, chan = maps_ref.shape
    slots = q_refs[0].shape[0]
    hid = coef_ref.shape[0] // 2
    part = 2 * TILE
    here = lax.axis_index("frame").astype(jnp.int32)
    query = q_refs[0][...]
    for ref in q_refs[1:]:
        query = query + ref[...]
    turned_q = query.T
    scale = 1.0 / math.sqrt(chan)

    for lo, hi in ((0, GRID_W), (GRID_W + pixels, ROWS_PAD * GRID_W)):
        cost_ref[lo:hi, :] = jnp.zeros((hi - lo, slots), F32)
        high_ref[lo:hi, :] = jnp.zeros((hi - lo, slots), BF16)
        low_ref[lo:hi, :] = jnp.zeros((hi - lo, slots), BF16)

    step = 512

    def cost_step(n):
        at = n * step
        block = maps_ref[pl.ds(at, step), :]
        if n < 2:
            cost = jnp.dot(block, turned_q, preferred_element_type=F32) * scale
        else:
            cost = lax.dot_general(
                query, block, (((1,), (1,)), ((), ())), preferred_element_type=F32
            )
            cost = cost.T * scale
        to = at + GRID_W
        high = cost.astype(BF16)
        cost_ref[pl.ds(to, step), :] = cost
        high_ref[pl.ds(to, step), :] = high
        low_ref[pl.ds(to, step), :] = (cost - high.astype(F32)).astype(BF16)

    cols = GRID_W // TILE
    def window_step(j, best):
        for k in range(cols):
            base = j * 4 * GRID_W + k * TILE
            left = (
                jnp.zeros((8, slots), F32)
                if k == 0
                else cost_ref[pl.ds(base - 1, 8, stride=GRID_W), :]
            )
            right = (
                jnp.zeros((8, slots), F32)
                if k == cols - 1
                else cost_ref[pl.ds(base + TILE, 8, stride=GRID_W), :]
            )
            both = jnp.concatenate([left, right], axis=0)
            high = both.astype(BF16)
            edge_high[k] = high
            edge_low[k] = (both - high.astype(F32)).astype(BF16)
        for parity in range(2):
            top = (4 * j + 2 * parity) * GRID_W
            for pair in range(cols // 2):
                sides = []
                for k in (2 * pair, 2 * pair + 1):
                    at = [top + rr * GRID_W + k * TILE for rr in range(4)]
                    mid_high = [high_ref[pl.ds(a, TILE), :] for a in at]
                    mid_low = [low_ref[pl.ds(a, TILE), :] for a in at]
                    eh, el = edge_high[k], edge_low[k]
                    sides.append(
                        jnp.concatenate(mid_high + mid_low + mid_high + [eh, el, eh, eh], axis=0)
                    )
                window = jnp.concatenate(sides, axis=1)
                cuts = 2 if j == GRID_H // 4 - 1 and parity == 1 and pair >= 0 else 1
                length = hid * part // cuts
                act = jnp.concatenate(
                    [
                        jnp.dot(
                            weight_ref[parity, n * length : (n + 1) * length],
                            window,
                            preferred_element_type=F32,
                        )
                        for n in range(cuts)
                    ],
                    axis=0,
                )
                for side in range(2):
                    k = 2 * pair + side
                    lanes = slice(side * slots, (side + 1) * slots)
                    for q in range(part // 8):
                        acc = coef_ref[2 * hid]
                        for h in range(hid):
                            at = h * part + 8 * q
                            acc = acc + coef_ref[hid + h] * jnp.maximum(
                                act[at : at + 8, lanes], coef_ref[h]
                            )
                        to = top + (8 * q // TILE) * GRID_W + k * TILE + 8 * q % TILE
                        logit_ref[pl.ds(to, 8), :] = acc
                        best = jnp.maximum(best, acc)
        return best

    def chunk_step(c, carry):
        best, row_acc, col_acc = carry
        peak = best
        for m in range(CHUNK // 4):
            peak = window_step(c * (CHUNK // 4) + m, peak)
        peak_ref[c] = peak
        shrink = jnp.exp2(best - peak)
        row_acc = row_acc * shrink
        col_acc = [part * shrink for part in col_acc]
        for m in range(CHUNK):
            r = c * CHUNK + m
            values = []
            for n in range(GRID_W // 8):
                at = r * GRID_W + 8 * n
                value = jnp.exp2(logit_ref[pl.ds(at, 8), :] - peak)
                logit_ref[pl.ds(at, 8), :] = value
                col_acc[n] = col_acc[n] + value
                values.append(value)
            while len(values) > 1:
                values = [x + y for x, y in zip(values[::2], values[1::2])]
            row_acc = row_acc + values[0] * (r * (1.0 / (GRID_H - 1)))
        return peak, row_acc, col_acc

    zero = jnp.zeros((8, slots), F32)
    carry = (jnp.full((8, slots), -jnp.inf, F32), zero, [zero] * (GRID_W // 8))
    cost_step(0)
    cost_step(1)
    for c in range(GRID_H // CHUNK):
        carry = chunk_step(c, carry)
        ahead_at = c // 2 + 2
        if c % 2 == 0 and ahead_at < pixels // step:
            cost_step(ahead_at)
    best, row_acc, col_acc = carry
    top_value = jnp.max(best, axis=0, keepdims=True)
    shrink = jnp.exp2(best - top_value)
    total, col_sum = zero, zero
    for n in range(GRID_W // 8):
        col_pos = (iota((8, slots), 0) + 8 * n).astype(F32) * (1.0 / (GRID_W - 1))
        total = total + col_acc[n]
        col_sum = col_sum + col_acc[n] * col_pos
    inverse = 1.0 / jnp.sum(total * shrink, axis=0, keepdims=True)
    row_est = jnp.sum(row_acc * shrink, axis=0, keepdims=True) * inverse
    col_est = jnp.sum(col_sum * shrink, axis=0, keepdims=True) * inverse

    span = CHUNK * GRID_W

    each = GRID_H // CHUNK

    def sample_step(n, sums):
        sums = list(sums)
        for m in range(each):
            c = n * each + m
            at = pl.multiple_of(c * span, span)
            factor = jnp.exp2(peak_ref[c] - top_value) * inverse
            heat = logit_ref[pl.ds(at, span), :].reshape(span // 8, 8, slots) * factor
            heat = heat.reshape(span, slots).astype(BF16)
            sums[m % 2] = sums[m % 2] + jnp.dot(
                heat.T, maps_ref[pl.ds(at, span), :], preferred_element_type=F32
            )
        return tuple(sums)

    sums = lax.fori_loop(
        0, lax.min(here, 0) + 1, sample_step, (jnp.zeros((slots, chan), F32),) * 2
    )
    sampled = sums[0] + sums[1]
    rest = jnp.concatenate([row_est, col_est, jnp.zeros((LANES - 2, slots), F32)], axis=0)
    sub = slots // pieces
    full_ref[:, :, :chan] = sampled.astype(BF16).reshape(pieces, sub, chan)
    full_ref[:, :, chan:] = rest.T.astype(BF16).reshape(pieces, sub, LANES)
    for m in range(pieces):
        out_refs[m][...] = full_ref[ahead(here, m, pieces)]


def mix_kernel(frames, *refs):
    got_refs = refs[:frames]
    mix_in_ref, taps_ref, gain_ref, mix_out_ref, out_ref, z_ref, join_ref = refs[frames:]
    chan = mix_in_ref.shape[0]
    rows = got_refs[0].shape[0]
    here = lax.axis_index("frame").astype(jnp.int32)
    for m in range(frames):
        join_ref[ahead(here, -m, frames)] = got_refs[m][...]
    joined = join_ref[...].reshape(frames * rows, join_ref.shape[2])
    place = joined[:, chan:].astype(F32).T[:8]
    z_ref[...] = jnp.dot(
        joined[:, :chan], mix_in_ref[...], preferred_element_type=F32
    ).reshape(z_ref.shape)
    rate = math.sqrt(2.0 / math.pi)
    hidden = []
    for t in range(frames):
        mixed = taps_ref[1:2, :] * z_ref[t]
        if t > 0:
            mixed = taps_ref[0:1, :] * z_ref[t - 1] + mixed
        if t < frames - 1:
            mixed = mixed + taps_ref[2:3, :] * z_ref[t + 1]
        power = jnp.mean(mixed * mixed, axis=-1, keepdims=True)
        normed = mixed * lax.rsqrt(power + 1e-06) * gain_ref[...]
        curve = jnp.tanh(normed * (normed * normed * (0.044715 * rate) + rate))
        half = 0.5 * normed
        hidden.append((half * curve + half).astype(BF16))
    delta = lax.dot_general(
        mix_out_ref[...],
        jnp.concatenate(hidden, axis=0),
        (((1,), (1,)), ((), ())),
        preferred_element_type=F32,
    )
    count = mix_out_ref.shape[0]
    result = delta + place[:count]
    for t in range(frames):
        out_ref[:, t, :] = result[:, t * rows : (t + 1) * rows]


def ahead(here, m, count):
    if isinstance(here, int):
        return (here + m) % count
    return lax.rem(here + m + count, count)


def in_hbm(x):
    return pltpu.with_memory_space_constraint(x, pltpu.MemorySpace.HBM)


def in_vmem(x):
    return pltpu.with_memory_space_constraint(x, pltpu.MemorySpace.VMEM)


def on_device(
    feature_maps,
    query_frame,
    query_row,
    query_col,
    track_order,
    conv_weight,
    conv_bias,
    head_weight,
    mix_in,
    temporal_taps,
    mix_gain,
    mix_out,
):
    frame_count = lax.axis_size("frame")
    track_count = lax.axis_size("track")
    f_dev, pixels, chan = feature_maps.shape
    total = track_order.shape[0]
    tr_dev = total // track_count
    sub_rows = tr_dev // frame_count
    hid = conv_weight.shape[0]
    mixw = mix_in.shape[1]
    maps = feature_maps.reshape(f_dev * pixels, chan)

    def send(x, m):
        pairs = [(i, ahead(i, m, frame_count)) for i in range(frame_count)]
        return lax.ppermute(x, "frame", pairs)

    def swap(x, m):
        return lax.ppermute(x, "frame", [(i, i ^ m) for i in range(frame_count)])

    limits = pltpu.CompilerParams(vmem_limit_bytes=24 << 20)
    any_spec = pl.BlockSpec(memory_space=pl.ANY)
    picks, held = pl.pallas_call(
        functools.partial(pick_kernel, frame_count, track_count),
        name="pick",
        out_shape=(pltpu.VMEM((tr_dev, chan), BF16), pltpu.VMEM((pixels, chan), BF16)),
        in_specs=[any_spec] * 5,
        out_specs=(VMEM_SPEC, VMEM_SPEC),
        scratch_shapes=[
            pltpu.VMEM((4, 1, total), jnp.int32),
            pltpu.SemaphoreType.DMA((4,)),
            pltpu.SemaphoreType.DMA((2,)),
        ],
        compiler_params=limits,
    )(
        in_hbm(track_order.reshape(1, total)),
        in_hbm(query_frame.reshape(1, total)),
        in_hbm(query_row.reshape(1, total)),
        in_hbm(query_col.reshape(1, total)),
        in_hbm(maps),
    )
    if frame_count & (frame_count - 1) == 0:
        others = [1, *range(frame_count - 1, 1, -1)]
        queries = [picks] + [swap(picks, m) for m in others]
    else:
        queries = [picks] + [send(picks, m) for m in range(1, frame_count)]

    part = 2 * TILE
    weight, coef = pl.pallas_call(
        prep_kernel,
        name="prep",
        out_shape=(
            pltpu.VMEM((2, hid * part, KDIM), BF16),
            pltpu.VMEM((2 * hid + 1, 8, tr_dev), F32),
        ),
        in_specs=[SMEM_SPEC] * 3,
        out_specs=(VMEM_SPEC, VMEM_SPEC),
        compiler_params=limits,
    )(conv_weight, conv_bias, head_weight)

    padded = ROWS_PAD * GRID_W
    pieces = pl.pallas_call(
        functools.partial(heat_kernel, frame_count, len(queries)),
        name="heat",
        out_shape=tuple(
            pltpu.VMEM((sub_rows, chan + LANES), BF16) for _ in range(frame_count)
        ),
        in_specs=[VMEM_SPEC] * (len(queries) + 3),
        out_specs=tuple(VMEM_SPEC for _ in range(frame_count)),
        scratch_shapes=[
            pltpu.VMEM((padded, tr_dev), F32),
            pltpu.VMEM((padded, tr_dev), BF16),
            pltpu.VMEM((padded, tr_dev), BF16),
            pltpu.VMEM((GRID_W // TILE, TILE, tr_dev), BF16),
            pltpu.VMEM((GRID_W // TILE, TILE, tr_dev), BF16),
            pltpu.VMEM((pixels, tr_dev), F32),
            pltpu.VMEM((GRID_H // CHUNK, 8, tr_dev), F32),
            pltpu.VMEM((frame_count, sub_rows, chan + LANES), BF16),
        ],
        compiler_params=limits,
    )(
        *[in_vmem(q) for q in queries],
        in_vmem(held),
        in_vmem(weight),
        in_vmem(coef),
    )
    got = [pieces[0]] + [send(pieces[m], m) for m in range(1, frame_count)]
    mixed = pl.pallas_call(
        functools.partial(mix_kernel, frame_count),
        name="mix",
        out_shape=jax.ShapeDtypeStruct((mix_out.shape[1], frame_count, sub_rows), F32),
        in_specs=[VMEM_SPEC] * (frame_count + 4),
        out_specs=VMEM_SPEC,
        scratch_shapes=[
            pltpu.VMEM((frame_count, sub_rows, mixw), F32),
            pltpu.VMEM((frame_count, sub_rows, chan + LANES), BF16),
        ],
        compiler_params=limits,
    )(
        *[in_vmem(g) for g in got],
        in_vmem(mix_in),
        in_vmem(temporal_taps),
        in_vmem(mix_gain.reshape(1, mixw)),
        in_vmem(mix_out.T),
    )
    return jnp.transpose(mixed, (2, 0, 1))


def solution(mesh):
    placed = (
        P(("clip", "frame"), None, None),
        P("clip"),
        P("clip"),
        P("clip"),
        P("clip"),
        P(),
        P(),
        P(),
        P(),
        P(),
        P(),
        P(),
    )
    return jax.shard_map(
        on_device,
        mesh=mesh,
        in_specs=placed,
        out_specs=P(("clip", "frame", "track"), None, None),
        check_vma=False,
    )
```

```python
import functools
import math

import jax
import jax.numpy as jnp
from jax import lax
from jax.experimental import pallas as pl
from jax.experimental.pallas import tpu as pltpu
from jax.sharding import PartitionSpec as P

GRID_H = 64
GRID_W = 64
TILE = 16
KDIM = 256
ROWS_PAD = GRID_H + 4
LANES = 128
CHUNK = 4
LOG2E = math.log2(math.e)

VMEM_SPEC = pl.BlockSpec(memory_space=pltpu.VMEM)
SMEM_SPEC = pl.BlockSpec(memory_space=pltpu.SMEM)
F32 = jnp.float32
BF16 = jnp.bfloat16


def iota(shape, dim):
    return lax.broadcasted_iota(jnp.int32, shape, dim)


def pick_kernel(
    frame_count,
    track_count,
    order_hbm,
    qf_hbm,
    qr_hbm,
    qc_hbm,
    maps_hbm,
    out_ref,
    held_ref,
    index_ref,
    index_sem,
    sem,
):
    total = order_hbm.shape[1]
    slots = out_ref.shape[0]
    pixels, chan = held_ref.shape
    chunks = sem.shape[0]
    step = pixels // chunks
    small = [
        pltpu.make_async_copy(src, index_ref.at[n], index_sem.at[n])
        for n, src in enumerate((order_hbm, qf_hbm, qr_hbm, qc_hbm))
    ]
    copies = [
        pltpu.make_async_copy(
            maps_hbm.at[pl.ds(n * step, step)], held_ref.at[pl.ds(n * step, step)], sem.at[n]
        )
        for n in range(chunks)
    ]
    for copy in small + copies:
        copy.start()
    frame_here = lax.axis_index("frame").astype(jnp.int32)
    track_here = lax.axis_index("track").astype(jnp.int32)
    sub = slots // frame_count
    at = iota((1, slots), 1)
    slot = (at // sub * track_count + track_here) * sub + at % sub
    row = iota((total, slots), 0)
    hot = jnp.where(row == slot, 1.0, 0.0).astype(BF16)
    for copy in small:
        copy.wait()
    order = index_ref[0]
    blank = jnp.zeros((5, total), jnp.int32)
    table = jnp.concatenate([order // 256, order % 256, blank, blank[:1]], axis=0)
    found = jnp.dot(table.astype(F32).astype(BF16), hot, preferred_element_type=F32)
    track = (found[0:1] * 256.0 + found[1:2]).astype(jnp.int32)
    hot = jnp.where(row == track, 1.0, 0.0).astype(BF16)
    table = jnp.concatenate([index_ref[1], index_ref[2], index_ref[3], blank], axis=0)
    found = jnp.dot(table.astype(F32).astype(BF16), hot, preferred_element_type=F32)
    flat = found[1:2] * GRID_W + found[2:3]
    flat = jnp.where(found[0:1] == frame_here.astype(F32), flat, -1.0)
    column = jnp.broadcast_to(flat, (slots, slots)).T[:, 0:1].astype(jnp.int32)
    half = step // 2
    spread = jnp.broadcast_to(column, (slots, half))
    lane = iota((slots, half), 1)
    sums = [jnp.zeros((slots, chan), F32)] * 2
    for n in range(chunks):
        copies[n].wait()
        for m in range(2):
            at = n * step + m * half
            sel = jnp.where(spread == lane + at, 1.0, 0.0).astype(BF16)
            sums[m] = sums[m] + jnp.dot(
                sel, held_ref[at : at + half, :], preferred_element_type=F32
            )
    out_ref[...] = (sums[0] + sums[1]).astype(BF16)


def prep_kernel(weight_ref, bias_ref, head_ref, out_ref, coef_ref):
    hid = weight_ref.shape[0]
    part = 2 * TILE
    row = iota((part, KDIM), 0)
    kk = iota((part, KDIM), 1)
    row_out, col_out = row // TILE, row % TILE
    mid = kk < 12 * TILE
    within = kk % (4 * TILE)
    seg = kk // (4 * TILE)
    edge = kk - 12 * TILE
    edge_seg = edge // TILE
    edge_at = edge % TILE
    use_low = jnp.where(mid, seg, edge_seg) == 2
    for parity in range(2):
        row_in = jnp.where(mid, within // TILE, edge_at % 8 - 2 * parity)
        col_in = jnp.where(mid, within % TILE, jnp.where(edge_at < 8, -1, TILE))
        down, across = row_in - row_out, col_in - col_out + 1
        good = (row_in >= 0) & (row_in < 4) & (down >= 0) & (down < 3)
        good = good & (across >= 0) & (across < 3) & (mid | (edge_seg < 3))
        tap = jnp.where(good, down * 3 + across, -1)
        masks = [tap == t for t in range(9)]
        for h in range(hid):
            full = jnp.zeros((part, KDIM), F32)
            for t in range(9):
                full = jnp.where(masks[t], weight_ref[h, t], full)
            high = full.astype(BF16).astype(F32)
            value = jnp.where(use_low, full - high, high)
            out_ref[parity, h * part : (h + 1) * part, :] = value.astype(BF16)
    const = 0.0
    for h in range(hid):
        coef_ref[h] = jnp.full(coef_ref.shape[1:], -bias_ref[h], F32)
        coef_ref[hid + h] = jnp.full(coef_ref.shape[1:], head_ref[h] * LOG2E, F32)
        const = const + head_ref[h] * bias_ref[h]
    coef_ref[2 * hid] = jnp.full(coef_ref.shape[1:], const * LOG2E, F32)


def heat_kernel(
    pieces,
    queries,
    *refs,
):
    q_refs = refs[:queries]
    maps_ref, weight_ref, coef_ref = refs[queries : queries + 3]
    rest = refs[queries + 3 :]
    out_refs = rest[:pieces]
    cost_ref, high_ref, low_ref, edge_high, edge_low, logit_ref, peak_ref, full_ref = rest[pieces:]
    pixels, chan = maps_ref.shape
    slots = q_refs[0].shape[0]
    hid = coef_ref.shape[0] // 2
    part = 2 * TILE
    here = lax.axis_index("frame").astype(jnp.int32)
    query = q_refs[0][...]
    for ref in q_refs[1:]:
        query = query + ref[...]
    turned_q = query.T
    scale = 1.0 / math.sqrt(chan)

    for lo, hi in ((0, GRID_W), (GRID_W + pixels, ROWS_PAD * GRID_W)):
        cost_ref[lo:hi, :] = jnp.zeros((hi - lo, slots), F32)
        high_ref[lo:hi, :] = jnp.zeros((hi - lo, slots), BF16)
        low_ref[lo:hi, :] = jnp.zeros((hi - lo, slots), BF16)

    step = 512

    def cost_step(n):
        at = n * step
        block = maps_ref[pl.ds(at, step), :]
        if n < 2:
            cost = jnp.dot(block, turned_q, preferred_element_type=F32) * scale
        else:
            cost = lax.dot_general(
                query, block, (((1,), (1,)), ((), ())), preferred_element_type=F32
            )
            cost = cost.T * scale
        to = at + GRID_W
        high = cost.astype(BF16)
        cost_ref[pl.ds(to, step), :] = cost
        high_ref[pl.ds(to, step), :] = high
        low_ref[pl.ds(to, step), :] = (cost - high.astype(F32)).astype(BF16)

    cols = GRID_W // TILE
    def window_step(j, best):
        for k in range(cols):
            base = j * 4 * GRID_W + k * TILE
            left = (
                jnp.zeros((8, slots), F32)
                if k == 0
                else cost_ref[pl.ds(base - 1, 8, stride=GRID_W), :]
            )
            right = (
                jnp.zeros((8, slots), F32)
                if k == cols - 1
                else cost_ref[pl.ds(base + TILE, 8, stride=GRID_W), :]
            )
            both = jnp.concatenate([left, right], axis=0)
            high = both.astype(BF16)
            edge_high[k] = high
            edge_low[k] = (both - high.astype(F32)).astype(BF16)
        for parity in range(2):
            top = (4 * j + 2 * parity) * GRID_W
            for pair in range(cols // 2):
                sides = []
                for k in (2 * pair, 2 * pair + 1):
                    at = [top + rr * GRID_W + k * TILE for rr in range(4)]
                    mid_high = [high_ref[pl.ds(a, TILE), :] for a in at]
                    mid_low = [low_ref[pl.ds(a, TILE), :] for a in at]
                    eh, el = edge_high[k], edge_low[k]
                    sides.append(
                        jnp.concatenate(mid_high + mid_low + mid_high + [eh, el, eh, eh], axis=0)
                    )
                window = jnp.concatenate(sides, axis=1)
                cuts = 2 if j == GRID_H // 4 - 1 and parity == 1 and pair >= 0 else 1
                length = hid * part // cuts
                act = jnp.concatenate(
                    [
                        jnp.dot(
                            weight_ref[parity, n * length : (n + 1) * length],
                            window,
                            preferred_element_type=F32,
                        )
                        for n in range(cuts)
                    ],
                    axis=0,
                )
                for side in range(2):
                    k = 2 * pair + side
                    lanes = slice(side * slots, (side + 1) * slots)
                    for q in range(part // 8):
                        acc = coef_ref[2 * hid]
                        for h in range(hid):
                            at = h * part + 8 * q
                            acc = acc + coef_ref[hid + h] * jnp.maximum(
                                act[at : at + 8, lanes], coef_ref[h]
                            )
                        to = top + (8 * q // TILE) * GRID_W + k * TILE + 8 * q % TILE
                        logit_ref[pl.ds(to, 8), :] = acc
                        best = jnp.maximum(best, acc)
        return best

    def chunk_step(c, carry):
        best, row_acc, col_acc = carry
        peak = best
        for m in range(CHUNK // 4):
            peak = window_step(c * (CHUNK // 4) + m, peak)
        peak_ref[c] = peak
        shrink = jnp.exp2(best - peak)
        row_acc = row_acc * shrink
        col_acc = [part * shrink for part in col_acc]
        for m in range(CHUNK):
            r = c * CHUNK + m
            values = []
            for n in range(GRID_W // 8):
                at = r * GRID_W + 8 * n
                value = jnp.exp2(logit_ref[pl.ds(at, 8), :] - peak)
                logit_ref[pl.ds(at, 8), :] = value
                col_acc[n] = col_acc[n] + value
                values.append(value)
            while len(values) > 1:
                values = [x + y for x, y in zip(values[::2], values[1::2])]
            row_acc = row_acc + values[0] * (r * (1.0 / (GRID_H - 1)))
        return peak, row_acc, col_acc

    zero = jnp.zeros((8, slots), F32)
    carry = (jnp.full((8, slots), -jnp.inf, F32), zero, [zero] * (GRID_W // 8))
    cost_step(0)
    for c in range(GRID_H // CHUNK):
        carry = chunk_step(c, carry)
        if c == 0:
            cost_step(1)
        ahead_at = c // 2 + 2
        if c % 2 == 0 and ahead_at < pixels // step:
            cost_step(ahead_at)
    best, row_acc, col_acc = carry
    top_value = jnp.max(best, axis=0, keepdims=True)
    shrink = jnp.exp2(best - top_value)
    total, col_sum = zero, zero
    for n in range(GRID_W // 8):
        col_pos = (iota((8, slots), 0) + 8 * n).astype(F32) * (1.0 / (GRID_W - 1))
        total = total + col_acc[n]
        col_sum = col_sum + col_acc[n] * col_pos
    inverse = 1.0 / jnp.sum(total * shrink, axis=0, keepdims=True)
    row_est = jnp.sum(row_acc * shrink, axis=0, keepdims=True) * inverse
    col_est = jnp.sum(col_sum * shrink, axis=0, keepdims=True) * inverse

    span = CHUNK * GRID_W

    each = GRID_H // CHUNK

    def sample_step(n, sums):
        sums = list(sums)
        for m in range(each):
            c = n * each + m
            at = pl.multiple_of(c * span, span)
            factor = jnp.exp2(peak_ref[c] - top_value) * inverse
            heat = logit_ref[pl.ds(at, span), :].reshape(span // 8, 8, slots) * factor
            heat = heat.reshape(span, slots).astype(BF16)
            sums[m % 2] = sums[m % 2] + jnp.dot(
                heat.T, maps_ref[pl.ds(at, span), :], preferred_element_type=F32
            )
        return tuple(sums)

    sums = lax.fori_loop(
        0, lax.min(here, 0) + 1, sample_step, (jnp.zeros((slots, chan), F32),) * 2
    )
    sampled = sums[0] + sums[1]
    rest = jnp.concatenate([row_est, col_est, jnp.zeros((LANES - 2, slots), F32)], axis=0)
    sub = slots // pieces
    full_ref[:, :, :chan] = sampled.astype(BF16).reshape(pieces, sub, chan)
    full_ref[:, :, chan:] = rest.T.astype(BF16).reshape(pieces, sub, LANES)
    for m in range(pieces):
        out_refs[m][...] = full_ref[ahead(here, m, pieces)]


def mix_kernel(frames, *refs):
    got_refs = refs[:frames]
    mix_in_ref, taps_ref, gain_ref, mix_out_ref, out_ref, z_ref, join_ref = refs[frames:]
    chan = mix_in_ref.shape[0]
    rows = got_refs[0].shape[0]
    here = lax.axis_index("frame").astype(jnp.int32)
    for m in range(frames):
        join_ref[ahead(here, -m, frames)] = got_refs[m][...]
    joined = join_ref[...].reshape(frames * rows, join_ref.shape[2])
    place = joined[:, chan:].astype(F32).T[:8]
    z_ref[...] = jnp.dot(
        joined[:, :chan], mix_in_ref[...], preferred_element_type=F32
    ).reshape(z_ref.shape)
    rate = math.sqrt(2.0 / math.pi)
    hidden = []
    for t in range(frames):
        mixed = taps_ref[1:2, :] * z_ref[t]
        if t > 0:
            mixed = taps_ref[0:1, :] * z_ref[t - 1] + mixed
        if t < frames - 1:
            mixed = mixed + taps_ref[2:3, :] * z_ref[t + 1]
        power = jnp.mean(mixed * mixed, axis=-1, keepdims=True)
        normed = mixed * lax.rsqrt(power + 1e-06) * gain_ref[...]
        curve = jnp.tanh(normed * (normed * normed * (0.044715 * rate) + rate))
        half = 0.5 * normed
        hidden.append((half * curve + half).astype(BF16))
    delta = lax.dot_general(
        mix_out_ref[...],
        jnp.concatenate(hidden, axis=0),
        (((1,), (1,)), ((), ())),
        preferred_element_type=F32,
    )
    count = mix_out_ref.shape[0]
    result = delta + place[:count]
    for t in range(frames):
        out_ref[:, t, :] = result[:, t * rows : (t + 1) * rows]


def ahead(here, m, count):
    if isinstance(here, int):
        return (here + m) % count
    return lax.rem(here + m + count, count)


def in_hbm(x):
    return pltpu.with_memory_space_constraint(x, pltpu.MemorySpace.HBM)


def in_vmem(x):
    return pltpu.with_memory_space_constraint(x, pltpu.MemorySpace.VMEM)


def on_device(
    feature_maps,
    query_frame,
    query_row,
    query_col,
    track_order,
    conv_weight,
    conv_bias,
    head_weight,
    mix_in,
    temporal_taps,
    mix_gain,
    mix_out,
):
    frame_count = lax.axis_size("frame")
    track_count = lax.axis_size("track")
    f_dev, pixels, chan = feature_maps.shape
    total = track_order.shape[0]
    tr_dev = total // track_count
    sub_rows = tr_dev // frame_count
    hid = conv_weight.shape[0]
    mixw = mix_in.shape[1]
    maps = feature_maps.reshape(f_dev * pixels, chan)

    def send(x, m):
        pairs = [(i, ahead(i, m, frame_count)) for i in range(frame_count)]
        return lax.ppermute(x, "frame", pairs)

    def swap(x, m):
        return lax.ppermute(x, "frame", [(i, i ^ m) for i in range(frame_count)])

    limits = pltpu.CompilerParams(vmem_limit_bytes=24 << 20)
    any_spec = pl.BlockSpec(memory_space=pl.ANY)
    picks, held = pl.pallas_call(
        functools.partial(pick_kernel, frame_count, track_count),
        name="pick",
        out_shape=(pltpu.VMEM((tr_dev, chan), BF16), pltpu.VMEM((pixels, chan), BF16)),
        in_specs=[any_spec] * 5,
        out_specs=(VMEM_SPEC, VMEM_SPEC),
        scratch_shapes=[
            pltpu.VMEM((4, 1, total), jnp.int32),
            pltpu.SemaphoreType.DMA((4,)),
            pltpu.SemaphoreType.DMA((2,)),
        ],
        compiler_params=limits,
    )(
        in_hbm(track_order.reshape(1, total)),
        in_hbm(query_frame.reshape(1, total)),
        in_hbm(query_row.reshape(1, total)),
        in_hbm(query_col.reshape(1, total)),
        in_hbm(maps),
    )
    if frame_count & (frame_count - 1) == 0:
        others = [1, *range(frame_count - 1, 1, -1)]
        queries = [picks] + [swap(picks, m) for m in others]
    else:
        queries = [picks] + [send(picks, m) for m in range(1, frame_count)]

    part = 2 * TILE
    weight, coef = pl.pallas_call(
        prep_kernel,
        name="prep",
        out_shape=(
            pltpu.VMEM((2, hid * part, KDIM), BF16),
            pltpu.VMEM((2 * hid + 1, 8, tr_dev), F32),
        ),
        in_specs=[SMEM_SPEC] * 3,
        out_specs=(VMEM_SPEC, VMEM_SPEC),
        compiler_params=limits,
    )(conv_weight, conv_bias, head_weight)

    padded = ROWS_PAD * GRID_W
    pieces = pl.pallas_call(
        functools.partial(heat_kernel, frame_count, len(queries)),
        name="heat",
        out_shape=tuple(
            pltpu.VMEM((sub_rows, chan + LANES), BF16) for _ in range(frame_count)
        ),
        in_specs=[VMEM_SPEC] * (len(queries) + 3),
        out_specs=tuple(VMEM_SPEC for _ in range(frame_count)),
        scratch_shapes=[
            pltpu.VMEM((padded, tr_dev), F32),
            pltpu.VMEM((padded, tr_dev), BF16),
            pltpu.VMEM((padded, tr_dev), BF16),
            pltpu.VMEM((GRID_W // TILE, TILE, tr_dev), BF16),
            pltpu.VMEM((GRID_W // TILE, TILE, tr_dev), BF16),
            pltpu.VMEM((pixels, tr_dev), F32),
            pltpu.VMEM((GRID_H // CHUNK, 8, tr_dev), F32),
            pltpu.VMEM((frame_count, sub_rows, chan + LANES), BF16),
        ],
        compiler_params=limits,
    )(
        *[in_vmem(q) for q in queries],
        in_vmem(held),
        in_vmem(weight),
        in_vmem(coef),
    )
    got = [pieces[0]] + [send(pieces[m], m) for m in range(1, frame_count)]
    mixed = pl.pallas_call(
        functools.partial(mix_kernel, frame_count),
        name="mix",
        out_shape=jax.ShapeDtypeStruct((mix_out.shape[1], frame_count, sub_rows), F32),
        in_specs=[VMEM_SPEC] * (frame_count + 4),
        out_specs=VMEM_SPEC,
        scratch_shapes=[
            pltpu.VMEM((frame_count, sub_rows, mixw), F32),
            pltpu.VMEM((frame_count, sub_rows, chan + LANES), BF16),
        ],
        compiler_params=limits,
    )(
        *[in_vmem(g) for g in got],
        in_vmem(mix_in),
        in_vmem(temporal_taps),
        in_vmem(mix_gain.reshape(1, mixw)),
        in_vmem(mix_out.T),
    )
    return jnp.transpose(mixed, (2, 0, 1))


def solution(mesh):
    placed = (
        P(("clip", "frame"), None, None),
        P("clip"),
        P("clip"),
        P("clip"),
        P("clip"),
        P(),
        P(),
        P(),
        P(),
        P(),
        P(),
        P(),
    )
    return jax.shard_map(
        on_device,
        mesh=mesh,
        in_specs=placed,
        out_specs=P(("clip", "frame", "track"), None, None),
        check_vma=False,
    )
```
